128 devices in a mesh: group: 32 (over x, z, y_hi), grid: 4 (over y_lo, core).
Axes of the slice: x: 4, y: 4 (y_hi: 2, y_lo: 2; y = y_hi * 2 + y_lo), z: 4, core: 2. Of those that a mesh axis runs over, the one named last changes fastest.
Arguments:
- stochastic: bfloat16 [1024, 32, 1024], P('group', 'grid'), may hold values from -6 to 6
- plane_map: int32 [32, 1024], P('group'), may hold values from 0 to 1023, each once within a row
- core_orbitals: bfloat16 [32, 512, 32, 1024], P('group', None, 'grid'), may hold values from -0.03125 to 0.03125
- potential: float32 [32, 32, 1024], P('group', 'grid'), may hold values from 0 to 0.4
Outputs:
- density: float32 [32, 32, 1024], P('group', 'grid')
- own_filtered: float32 [1024, 32, 1024], P('group', 'grid')
The draws below stay inside these ranges and needn't reach their ends.
Inputs may be any that keep to these rules, and one draw needn't show every extreme that they name: `plane_map`: each row names every plane point once.
All inputs are finite; a program needn't handle non-finite values.
Results may differ from the reference program's by a relative error of at most 0.001.
Values may be sent and summed in bfloat16 or wider, within the bound.
No kernel may reach another device: no remote copies, remote signals or barrier semaphores. Data moves between devices by JAX's collectives and lax.ppermute only.
A program may use at most 128 MiB of HBM per device.

```python
import jax
import jax.numpy as jnp
from jax import lax

NCORE = 512
BY = 32
BZ = 32
BATCH = 32
KDEG = 6
NGROUPS = 32
BX = 32
PLANE = 1024
S = 1024


def block_scale(key, dims, cuts, low, top_value):
    loudness = 1.0
    for position, blocks in cuts:
        steps = jax.random.uniform(jax.random.fold_in(jax.random.fold_in(key, 6), position), (blocks,), jnp.float32, low / len(cuts), top_value / len(cuts))
        loudness = loudness * jnp.repeat(jnp.exp(steps), dims[position] // blocks).reshape((-1,) + (1,) * (len(dims) - 1 - position))
    return loudness


def centred(own_key, dims, width, most, split=(), kind=jnp.bfloat16):
    result = jax.random.normal(own_key, dims, jnp.float32) * width
    if len(split) > 0:
        result = block_scale(own_key, dims, split, -0.22, 0.18) * result
    return jnp.clip(result, min=-most, max=most).astype(kind)


def setup_inputs(seed: int = 0) -> dict:
    arg_keys = jax.random.split(jax.random.key(seed), 5)
    return {
        "stochastic": centred(arg_keys[0], (S, BX, PLANE), 1.0, 6.0, ((0, 32), (1, 4))),
        "plane_map": jax.vmap(lambda own: jax.random.permutation(own, PLANE))(jax.random.split(arg_keys[1], NGROUPS)).reshape((NGROUPS, PLANE)).astype(jnp.int32),
        "core_orbitals": centred(arg_keys[2], (NGROUPS, NCORE, BX, PLANE), (BX * PLANE) ** -0.5, 0.03125, ((0, 32), (2, 4))),
        "potential": jnp.clip(0.4 * jax.random.uniform(arg_keys[3], (NGROUPS, BX, PLANE), jnp.float32) ** block_scale(arg_keys[3], (NGROUPS, BX, PLANE), ((0, 32), (1, 4)), -0.2, 0.2), 0.0, 0.4),
    }


def hamiltonian(field, potential):
    padded_x = jnp.pad(field, ((0, 0), (1, 1), (0, 0)))
    beside = padded_x[:, 2:] + padded_x[:, :-2]
    padded_y = jnp.pad(field, ((0, 0), (0, 0), (BZ, BZ)))
    beside = beside + padded_y[:, :, 2 * BZ:] + padded_y[:, :, :-2 * BZ]
    padded_z = jnp.pad(field, ((0, 0), (0, 0), (1, 1)))
    zpos = jnp.arange(BY * BZ) % BZ
    beside = beside + jnp.where(zpos < BZ - 1, padded_z[:, :, 2:], 0.0)
    beside = beside + jnp.where(zpos > 0, padded_z[:, :, :-2], 0.0)
    return (6.0 * field - beside) / 8.0 + (potential - 1.0) * field


def visit(mapped, core_rows, potential):
    rows = mapped.shape[0]
    flat = mapped.reshape(rows, -1)
    coeffs = lax.dot_general(flat, core_rows, (((1,), (1,)), ((), ())), preferred_element_type=jnp.float32).astype(jnp.bfloat16)
    projected = (flat.astype(jnp.float32) - jnp.dot(coeffs, core_rows, preferred_element_type=jnp.float32)).reshape(mapped.shape)
    previous = projected
    current = hamiltonian(projected, potential)
    total = projected + current / 2.0
    for order in range(2, KDEG + 1):
        following = 2.0 * hamiltonian(current, potential) - previous
        total = total + following / (order + 1.0)
        previous, current = current, following
    rounded = total.astype(jnp.bfloat16).reshape(rows, -1)
    ends = lax.dot_general(rounded, core_rows, (((1,), (1,)), ((), ())), preferred_element_type=jnp.float32).astype(jnp.bfloat16)
    return total - jnp.dot(ends, core_rows, preferred_element_type=jnp.float32).reshape(mapped.shape)


def reference(stochastic, plane_map, core_orbitals, potential):
    batches = stochastic.reshape(NGROUPS, BATCH, BX, BY * BZ)

    def one_group(group_index):
        index_row = plane_map[group_index]
        core_rows = core_orbitals[group_index].reshape(NCORE, -1)
        local_potential = potential[group_index]
        accum = jnp.zeros((BX, BY * BZ), jnp.float32)
        first = None
        for visit_index in range(3):
            batch_index = (group_index - visit_index) % NGROUPS
            mapped = jnp.take(batches[batch_index], index_row, axis=2)
            cleaned = visit(mapped, core_rows, local_potential)
            accum = accum + jnp.sum(mapped.astype(jnp.float32) * cleaned, axis=0)
            if visit_index == 0:
                first = cleaned
        return accum / (3.0 * BATCH), first

    density, firsts = lax.map(one_group, jnp.arange(NGROUPS, dtype=jnp.int32))
    return density, firsts.reshape(NGROUPS * BATCH, BX, BY * BZ)
```

```python
from fractions import Fraction

import jax
import jax.numpy as jnp
from jax import lax
from jax.experimental import pallas as pl
from jax.experimental.pallas import tpu as pltpu
from jax.sharding import PartitionSpec as P

BZ = 32
KDEG = 6
BATCH = 32
NCORE = 512
SLAB = 8
PLANE = 1024
GRID = 4
HALO = KDEG
WIDE = SLAB + 2 * HALO
LANES = 128
TILES = PLANE // LANES
F32 = jnp.float32
BF16 = jnp.bfloat16


def horner_coefficients():
    cheb = [[Fraction(1)], [Fraction(0), Fraction(1)]]
    for _ in range(2, KDEG + 1):
        last, before = cheb[-1], cheb[-2]
        nxt = [Fraction(0)] + [2 * v for v in last]
        for i, v in enumerate(before):
            nxt[i] -= v
        cheb.append(nxt)
    mono = [Fraction(0)] * (KDEG + 1)
    for k, poly in enumerate(cheb):
        for i, v in enumerate(poly):
            mono[i] += v / (k + 1)
    scaled = [v / Fraction(-8) ** i for i, v in enumerate(mono)]
    top = scaled[KDEG]
    return [float(v / top) for v in scaled], float(top)


EK, TOP = horner_coefficients()


def row_permutation(rows, inner):
    outer = rows // inner
    out = lax.broadcasted_iota(jnp.int32, (rows, rows), 0)
    src = lax.broadcasted_iota(jnp.int32, (rows, rows), 1)
    return jnp.where(src == (out % outer) * inner + out // outer, 1.0, 0.0).astype(BF16)


def relayout_kernel(core_ref, out_ref, perm):
    @pl.when(pl.program_id(0) == 0)
    def _():
        perm[...] = row_permutation(256, SLAB)

    block = jnp.dot(perm[...], core_ref[...], preferred_element_type=F32)
    out_ref[...] = block.astype(BF16).reshape(SLAB, 32, PLANE)


def relayout(core):
    return pl.pallas_call(
        relayout_kernel,
        grid=(NCORE // 32,),
        in_specs=[pl.BlockSpec((256, PLANE), lambda i: (i, 0))],
        out_specs=pl.BlockSpec((SLAB, 32, PLANE), lambda i: (0, i, 0)),
        out_shape=jax.ShapeDtypeStruct((SLAB, NCORE, PLANE), BF16),
        scratch_shapes=[pltpu.VMEM((256, 256), BF16)],
        name="relayout",
    )(core.reshape(NCORE * SLAB, PLANE))


def map_kernel(*refs):
    index_ref, refs, out_ref, pick = refs[0], refs[1:-2], refs[-2], refs[-1]
    src = lax.broadcasted_iota(jnp.int32, (PLANE, PLANE), 0)
    pick[...] = jnp.where(src == index_ref[...], 1.0, 0.0).astype(BF16)
    perm = row_permutation(BATCH * SLAB, SLAB)
    for b, ref in enumerate(refs):
        rows = jnp.dot(perm, ref[...], preferred_element_type=F32).astype(BF16)
        got = jnp.dot(rows, pick[...], preferred_element_type=F32).astype(BF16)
        out_ref[:, b * BATCH : (b + 1) * BATCH, :] = got.reshape(SLAB, BATCH, PLANE)


def map_batches(index_row, batches):
    return pl.pallas_call(
        map_kernel,
        out_shape=jax.ShapeDtypeStruct((SLAB, BATCH * len(batches), PLANE), BF16),
        scratch_shapes=[pltpu.VMEM((PLANE, PLANE), BF16)],
        name="map_batches",
    )(index_row, *[b.reshape(BATCH * SLAB, PLANE) for b in batches])


def overlap_kernel(field_ref, core_ref, full_ref, half_ref):
    part = lax.dot_general(
        field_ref[0], core_ref[0], (((1,), (1,)), ((), ())), preferred_element_type=F32
    )
    x = pl.program_id(0)

    @pl.when(x == 0)
    def _():
        full_ref[...] = part

    @pl.when(x > 0)
    def _():
        full_ref[...] += part

    @pl.when(x == SLAB - 1)
    def _():
        half_ref[...] = full_ref[...].astype(BF16)


def overlap(field, core_x):
    rows = field.shape[1]
    whole = pl.BlockSpec((rows, NCORE), lambda x: (0, 0))
    return pl.pallas_call(
        overlap_kernel,
        grid=(SLAB,),
        in_specs=[
            pl.BlockSpec((1, rows, PLANE), lambda x: (x, 0, 0)),
            pl.BlockSpec((1, NCORE, PLANE), lambda x: (x, 0, 0)),
        ],
        out_specs=(whole, whole),
        out_shape=(
            jax.ShapeDtypeStruct((rows, NCORE), F32),
            jax.ShapeDtypeStruct((rows, NCORE), BF16),
        ),
        name="overlap",
    )(field, core_x)


def exchange(half):
    return [
        lax.ppermute(half, "grid", [(i, i ^ k) for i in range(GRID)]) for k in range(1, GRID)
    ]


def total_of(full_ref, a_ref, b_ref, c_ref):
    rest = a_ref[...].astype(F32) + b_ref[...].astype(F32) + c_ref[...].astype(F32)
    return (full_ref[...] + rest).astype(BF16)


def project_kernel(full_ref, a_ref, b_ref, c_ref, field_ref, core_ref, out_ref, low_ref, high_ref, coef):
    x = pl.program_id(0)

    @pl.when(x == 0)
    def _():
        coef[...] = total_of(full_ref, a_ref, b_ref, c_ref)

    value = field_ref[0].astype(F32) - jnp.dot(coef[...], core_ref[0], preferred_element_type=F32)
    out_ref[0] = value
    short = value.astype(BF16)

    @pl.when(x < HALO)
    def _():
        low_ref[0] = short

    high_ref[0] = short


def project(full, others, field, core_x):
    rows = field.shape[1]
    whole = pl.BlockSpec((rows, NCORE), lambda x: (0, 0))
    plane = pl.BlockSpec((1, rows, PLANE), lambda x: (x, 0, 0))
    return pl.pallas_call(
        project_kernel,
        grid=(SLAB,),
        in_specs=[whole] * 4 + [plane, pl.BlockSpec((1, NCORE, PLANE), lambda x: (x, 0, 0))],
        out_specs=(
            plane,
            pl.BlockSpec((1, rows, PLANE), lambda x: (jnp.minimum(x, HALO - 1), 0, 0)),
            pl.BlockSpec((1, rows, PLANE), lambda x: (jnp.maximum(x - (SLAB - HALO), 0), 0, 0)),
        ),
        out_shape=(
            jax.ShapeDtypeStruct((SLAB, rows, PLANE), F32),
            jax.ShapeDtypeStruct((HALO, rows, PLANE), BF16),
            jax.ShapeDtypeStruct((HALO, rows, PLANE), BF16),
        ),
        scratch_shapes=[pltpu.VMEM((rows, NCORE), BF16)],
        name="project",
    )(full, *others, field, core_x)


UP = [(i, i + 1) for i in range(GRID - 1)]
DOWN = [(j, i) for i, j in UP]


def filter_kernel(inside_ref, field_ref, below_ref, above_ref, weight_ref, core_hbm, out_ref, full_ref, half_ref, start, even, odd, rounded, core_x, sem):
    step = pl.program_id(0)
    fetch = pltpu.make_async_copy(core_hbm, core_x, sem)

    @pl.when(step == 0)
    def _():
        fetch.start()

    rows = field_ref.shape[1]
    lane = lax.broadcasted_iota(jnp.int32, (8, LANES), 1)
    first_y, last_y = lane < BZ, lane >= LANES - BZ
    first_z, last_z = lane % BZ == 0, lane % BZ == BZ - 1
    zero = jnp.zeros((8, LANES), F32)
    low_flag, high_flag = inside_ref[0], inside_ref[1]

    start[:HALO] = below_ref[...].astype(F32)
    start[HALO : HALO + SLAB] = field_ref[...]
    start[HALO + SLAB :] = above_ref[...].astype(F32)

    def tiles(ref, x, s):
        return [ref[x, s, pl.ds(j * LANES, LANES)] for j in range(TILES)]

    for block in range(rows // 8):
        s = pl.ds(block * 8, 8)
        source, local = start, s
        for k in range(1, KDEG + 1):
            target = even if k % 2 == 0 else odd
            first, last = k, WIDE - k
            here, after = tiles(source, first - 1, local), tiles(source, first, local)
            for x in range(first, last):
                before, here = here, after
                after = tiles(source, x + 1, local)
                for j in range(TILES):
                    lanes = pl.ds(j * LANES, LANES)
                    c = here[j]
                    nxt = here[j + 1] if j < TILES - 1 else zero
                    prv = here[j - 1] if j > 0 else zero
                    ys = pltpu.roll(jnp.where(first_y, nxt, c), LANES - BZ, 1) + pltpu.roll(
                        jnp.where(last_y, prv, c), BZ, 1
                    )
                    zs = pltpu.roll(jnp.where(last_z, 0.0, c), 1, 1) + pltpu.roll(
                        jnp.where(first_z, 0.0, c), LANES - 1, 1
                    )
                    around = (before[j] + after[j]) + (ys + zs)
                    w = jnp.broadcast_to(weight_ref[pl.ds(x, 1), lanes], (8, LANES))
                    value = around - w * c + EK[KDEG - k] * start[x, s, lanes]
                    if x < HALO:
                        value = value * low_flag
                    elif x >= HALO + SLAB:
                        value = value * high_flag
                    if k == KDEG:
                        out_ref[x - HALO, s, lanes] = value * TOP
                    else:
                        target[x, :, lanes] = value
            source, local = target, slice(None)

    rounded[:, pl.ds(step * rows, rows), :] = out_ref[...].astype(BF16)

    @pl.when(step == pl.num_programs(0) - 1)
    def _():
        fetch.wait()
        for x in range(SLAB):
            part = lax.dot_general(
                rounded[x], core_x[x], (((1,), (1,)), ((), ())), preferred_element_type=F32
            )
            if x == 0:
                full_ref[...] = part
            else:
                full_ref[...] += part
        half_ref[...] = full_ref[...].astype(BF16)


def chebyshev(inside, field, below, above, weight, core_x, block=16):
    rows = field.shape[1]
    spec = lambda n: pl.BlockSpec((n, block, PLANE), lambda i: (0, i, 0))
    whole = pl.BlockSpec((rows, NCORE), lambda i: (0, 0))
    return pl.pallas_call(
        filter_kernel,
        grid=(rows // block,),
        in_specs=[
            pl.BlockSpec(memory_space=pltpu.SMEM),
            spec(SLAB),
            spec(HALO),
            spec(HALO),
            pl.BlockSpec((WIDE, PLANE), lambda i: (0, 0)),
            pl.BlockSpec(memory_space=pl.ANY),
        ],
        out_specs=(spec(SLAB), whole, whole),
        out_shape=(
            jax.ShapeDtypeStruct((SLAB, rows, PLANE), F32),
            jax.ShapeDtypeStruct((rows, NCORE), F32),
            jax.ShapeDtypeStruct((rows, NCORE), BF16),
        ),
        scratch_shapes=[
            pltpu.VMEM((WIDE, block, PLANE), F32),
            pltpu.VMEM((WIDE, 8, PLANE), F32),
            pltpu.VMEM((WIDE, 8, PLANE), F32),
            pltpu.VMEM((SLAB, rows, PLANE), BF16),
            pltpu.VMEM((SLAB, NCORE, PLANE), BF16),
            pltpu.SemaphoreType.DMA,
        ],
        name="chebyshev",
    )(inside, field, below, above, weight, core_x)


def clean_kernel(full_ref, a_ref, b_ref, c_ref, field_ref, mapped_ref, core_ref, own_ref, density_ref, coef):
    x = pl.program_id(0)

    @pl.when(x == 0)
    def _():
        coef[...] = total_of(full_ref, a_ref, b_ref, c_ref)

    value = field_ref[0] - jnp.dot(coef[...], core_ref[0], preferred_element_type=F32)
    own_ref[0] = value[:BATCH]
    weighted = jnp.sum(mapped_ref[0].astype(F32) * value, axis=0, keepdims=True)
    density_ref[pl.ds(x, 1), :] = weighted / (3.0 * BATCH)


def clean(full, others, field, mapped, core_x):
    rows = field.shape[1]
    whole = pl.BlockSpec((rows, NCORE), lambda x: (0, 0))
    plane = pl.BlockSpec((1, rows, PLANE), lambda x: (x, 0, 0))
    return pl.pallas_call(
        clean_kernel,
        grid=(SLAB,),
        in_specs=[whole] * 4 + [plane, plane, pl.BlockSpec((1, NCORE, PLANE), lambda x: (x, 0, 0))],
        out_specs=(
            pl.BlockSpec((1, BATCH, PLANE), lambda x: (x, 0, 0)),
            pl.BlockSpec((SLAB, PLANE), lambda x: (0, 0)),
        ),
        out_shape=(
            jax.ShapeDtypeStruct((SLAB, BATCH, PLANE), F32),
            jax.ShapeDtypeStruct((SLAB, PLANE), F32),
        ),
        scratch_shapes=[pltpu.VMEM((rows, NCORE), BF16)],
        name="clean",
    )(full, *others, field, mapped, core_x)


def shifted(array, by):
    devices = lax.axis_size("group")
    return lax.ppermute(array, "group", [(i, (i + by) % devices) for i in range(devices)])


def body(stochastic, plane_map, core_orbitals, potential):
    third = shifted(stochastic, 2)
    second = shifted(stochastic, 1)
    local = potential[0]
    below_v = lax.ppermute(local[SLAB - HALO :], "grid", UP)
    above_v = lax.ppermute(local[:HALO], "grid", DOWN)
    weight = 8.0 * jnp.concatenate([below_v, local, above_v], axis=0) - 2.0
    place = lax.axis_index("grid")
    inside = jnp.stack([place > 0, place < GRID - 1]).astype(F32)

    core_x = relayout(core_orbitals[0])
    mapped = map_batches(plane_map, (stochastic, second, third))
    full, half = overlap(mapped, core_x)
    field, low, high = project(full, exchange(half), mapped, core_x)
    below = lax.ppermute(high, "grid", UP)
    above = lax.ppermute(low, "grid", DOWN)
    filtered, full, half = chebyshev(inside, field, below, above, weight, core_x)
    own, density = clean(full, exchange(half), filtered, mapped, core_x)
    return density[None], own.transpose(1, 0, 2)


def solution(mesh):
    return jax.shard_map(
        body,
        mesh=mesh,
        in_specs=(
            P("group", "grid", None),
            P("group", None),
            P("group", None, "grid", None),
            P("group", "grid", None),
        ),
        out_specs=(P("group", "grid", None), P("group", "grid", None)),
        check_vma=False,
    )
```

```python
from fractions import Fraction

import jax
import jax.numpy as jnp
from jax import lax
from jax.experimental import pallas as pl
from jax.experimental.pallas import tpu as pltpu
from jax.sharding import PartitionSpec as P

BZ = 32
KDEG = 6
BATCH = 32
NCORE = 512
SLAB = 8
PLANE = 1024
GRID = 4
HALO = KDEG
WIDE = SLAB + 2 * HALO
LANES = 128
TILES = PLANE // LANES
F32 = jnp.float32
BF16 = jnp.bfloat16


def horner_coefficients():
    cheb = [[Fraction(1)], [Fraction(0), Fraction(1)]]
    for _ in range(2, KDEG + 1):
        last, before = cheb[-1], cheb[-2]
        nxt = [Fraction(0)] + [2 * v for v in last]
        for i, v in enumerate(before):
            nxt[i] -= v
        cheb.append(nxt)
    mono = [Fraction(0)] * (KDEG + 1)
    for k, poly in enumerate(cheb):
        for i, v in enumerate(poly):
            mono[i] += v / (k + 1)
    scaled = [v / Fraction(-8) ** i for i, v in enumerate(mono)]
    top = scaled[KDEG]
    return [float(v / top) for v in scaled], float(top)


EK, TOP = horner_coefficients()

VMEM = pl.BlockSpec(memory_space=pltpu.VMEM)
MIB = 1 << 20
PIECE = 32
CHUNKS = NCORE // PIECE
NT = (((1,), (1,)), ((), ()))


def call(kernel, name, out_shape, in_specs, scratch=(), limit=8):
    return pl.pallas_call(
        kernel,
        in_specs=in_specs,
        out_specs=jax.tree.map(lambda _: VMEM, out_shape),
        out_shape=out_shape,
        scratch_shapes=list(scratch),
        compiler_params=pltpu.CompilerParams(vmem_limit_bytes=limit * MIB),
        name=name,
    )


def struct(shape, dtype):
    return jax.ShapeDtypeStruct(shape, dtype)


def one_hot(condition):
    return jnp.where(condition, 1.0, 0.0).astype(BF16)


def iota(shape, axis):
    return lax.broadcasted_iota(jnp.int32, shape, axis)


def dot(a, b):
    return jnp.dot(a, b, preferred_element_type=F32)


def dot_nt(a, b):
    return lax.dot_general(a, b, NT, preferred_element_type=F32)


def row_permutation(rows, inner):
    outer = rows // inner
    out, src = iota((rows, rows), 0), iota((rows, rows), 1)
    return one_hot(src == (out % outer) * inner + out // outer)


def natural_point(q):
    tile, lane = q // LANES, q % LANES
    return (4 * (lane // 16) + tile // 2) * BZ + 2 * (lane % 16) + tile % 2


def prepare_kernel(index_ref, local_ref, below_ref, above_ref, order_ref, index_out, weight_out):
    order = one_hot(iota((PLANE, PLANE), 1) == natural_point(iota((PLANE, PLANE), 0)))
    order_ref[...] = order
    index = index_ref[...]
    digits = jnp.concatenate([index // 32, index % 32] + [jnp.zeros((6, PLANE), jnp.int32)], axis=0)
    moved = dot_nt(digits.astype(F32).astype(BF16), order)
    index_out[...] = (moved[0:1] * 32.0 + moved[1:2]).astype(jnp.int32)
    for first, ref in ((0, below_ref), (HALO, local_ref), (HALO + SLAB, above_ref)):
        rest = ref[...]
        total = None
        for _ in range(3):
            part = rest.astype(BF16)
            rest = rest - part.astype(F32)
            moved = dot_nt(part, order)
            total = moved if total is None else total + moved
        weight_out[first : first + ref.shape[0]] = 8.0 * total - 2.0


def prepare(plane_map, local, below, above):
    return call(
        prepare_kernel,
        "prepare",
        (
            struct((PLANE, PLANE), BF16),
            struct((1, PLANE), jnp.int32),
            struct((WIDE, PLANE), F32),
        ),
        [VMEM] * 4,
    )(plane_map, local, below, above)


def relayout_kernel(core_ref, out_ref, mid):
    rows = row_permutation(256, SLAB)
    src, out = iota((256, 256), 0), iota((256, 256), 1)
    piece, low = out // PIECE, out % PIECE
    columns = one_hot(src == (4 * (low // 16) + piece // 2) * BZ + 2 * (low % 16) + piece % 2)
    lane = iota((PIECE, LANES), 1)
    half, quarter = lane < 64, lane % 64 < 32

    @pl.loop(0, CHUNKS)
    def _(i):
        block = pl.ds(pl.multiple_of(i * 256, 256), 256)
        for b in range(4):
            cols = pl.ds(b * 256, 256)
            ordered = dot(rows, core_ref[block, cols]).astype(BF16)
            mid[:, cols] = dot(ordered, columns).astype(BF16)
        at = pl.ds(pl.multiple_of(i * PIECE, PIECE), PIECE)
        for x in range(SLAB):
            for h in range(2):
                p = [
                    mid[pl.ds(x * PIECE, PIECE), pl.ds(b * 256 + h * LANES, LANES)].astype(F32)
                    for b in range(4)
                ]
                u = [jnp.where(half, p[k], pltpu.roll(p[k + 2], 64, 1)) for k in range(2)]
                v = [jnp.where(half, pltpu.roll(p[k], 64, 1), p[k + 2]) for k in range(2)]
                for k, (a, c) in enumerate((u, v)):
                    first = jnp.where(quarter, a, pltpu.roll(c, 32, 1))
                    second = jnp.where(quarter, pltpu.roll(a, LANES - 32, 1), c)
                    j = 4 * h + 2 * k
                    out_ref[x, at, pl.ds(j * LANES, LANES)] = first.astype(BF16)
                    out_ref[x, at, pl.ds((j + 1) * LANES, LANES)] = second.astype(BF16)


def relayout(core):
    return call(
        relayout_kernel,
        "relayout",
        struct((SLAB, NCORE, PLANE), BF16),
        [VMEM],
        [pltpu.VMEM((256, PLANE), BF16)],
    )(core.reshape(NCORE * SLAB, PLANE))


def sums(field_of, core_ref, full_ref, half_ref):
    for x in range(SLAB):
        part = dot_nt(field_of(x), core_ref[x])
        if x == 0:
            full_ref[...] = part
        else:
            full_ref[...] += part
    half_ref[...] = full_ref[...].astype(BF16)


def map_kernel(*refs):
    index_ref, core_ref, batches = refs[0], refs[1], refs[2:-4]
    out_ref, full_ref, half_ref, pick = refs[-4:]
    pick[...] = one_hot(iota((PLANE, PLANE), 0) == index_ref[...])
    perm = row_permutation(BATCH * SLAB, SLAB)
    for b, ref in enumerate(batches):
        rows = dot(perm, ref[...]).astype(BF16)
        got = dot(rows, pick[...]).astype(BF16)
        out_ref[:, b * BATCH : (b + 1) * BATCH, :] = got.reshape(SLAB, BATCH, PLANE)
    sums(lambda x: out_ref[x], core_ref, full_ref, half_ref)


def map_batches(index_row, core_x, batches):
    rows = BATCH * len(batches)
    return call(
        map_kernel,
        "map_batches",
        (struct((SLAB, rows, PLANE), BF16), struct((rows, NCORE), F32), struct((rows, NCORE), BF16)),
        [VMEM] * (2 + len(batches)),
        [pltpu.VMEM((PLANE, PLANE), BF16)],
        limit=12,
    )(index_row, core_x, *[b.reshape(BATCH * SLAB, PLANE) for b in batches])


def exchange(half):
    return [
        lax.ppermute(half, "grid", [(i, i ^ k) for i in range(GRID)]) for k in range(1, GRID)
    ]


def total_of(full_ref, a_ref, b_ref, c_ref):
    rest = a_ref[...].astype(F32) + b_ref[...].astype(F32) + c_ref[...].astype(F32)
    return (full_ref[...] + rest).astype(BF16)


def project_kernel(full_ref, a_ref, b_ref, c_ref, field_ref, core_ref, out_ref, low_ref, high_ref):
    coef = total_of(full_ref, a_ref, b_ref, c_ref)
    for x in range(SLAB):
        value = field_ref[x].astype(F32) - dot(coef, core_ref[x])
        out_ref[x] = value
        short = value.astype(BF16)
        if x < HALO:
            low_ref[x] = short
        if x >= SLAB - HALO:
            high_ref[x - (SLAB - HALO)] = short


def project(full, others, field, core_x):
    rows = field.shape[1]
    return call(
        project_kernel,
        "project",
        (
            struct((SLAB, rows, PLANE), F32),
            struct((HALO, rows, PLANE), BF16),
            struct((HALO, rows, PLANE), BF16),
        ),
        [VMEM] * 6,
    )(full, *others, field, core_x)


UP = [(i, i + 1) for i in range(GRID - 1)]
DOWN = [(j, i) for i, j in UP]


def filter_kernel(inside_ref, field_ref, below_ref, above_ref, weight_ref, core_ref, out_ref, full_ref, half_ref, start, even, odd):
    rows = field_ref.shape[1]
    lane = iota((8, LANES), 1)
    head, tail = lane < 16, lane >= LANES - 16
    first_z, last_z = lane % 16 == 0, lane % 16 == 15
    low_flag, high_flag = inside_ref[0], inside_ref[1]

    def tiles(ref, x, s):
        return [ref[x, s, pl.ds(j * LANES, LANES)] for j in range(TILES)]

    def rolled(mask, value, by):
        return pltpu.roll(jnp.where(mask, 0.0, value), by % LANES, 1)

    def sweep(s):
        source, local = start, s
        for k in range(1, KDEG + 1):
            target = even if k % 2 == 0 else odd
            first, last = k, WIDE - k
            here, after = tiles(source, first - 1, local), tiles(source, first, local)
            for x in range(first, last):
                before, here = here, after
                after = tiles(source, x + 1, local)
                up = [rolled(head, here[j], -16) for j in range(2)]
                down = [rolled(tail, here[j], 16) for j in range(6, 8)]
                for j in range(TILES):
                    lanes = pl.ds(j * LANES, LANES)
                    c = here[j]
                    above_y = here[j + 2] if j < 6 else up[j - 6]
                    below_y = here[j - 2] if j > 1 else down[j]
                    mate = here[j ^ 1]
                    z = mate + (rolled(first_z, mate, -1) if j % 2 else rolled(last_z, mate, 1))
                    around = (before[j] + after[j]) + (above_y + below_y) + z
                    w = jnp.broadcast_to(weight_ref[pl.ds(x, 1), lanes], (8, LANES))
                    value = around - w * c + EK[KDEG - k] * start[x, s, lanes]
                    if x < HALO:
                        value = value * low_flag
                    elif x >= HALO + SLAB:
                        value = value * high_flag
                    if k == KDEG:
                        target[x, :, lanes] = value * TOP
                    else:
                        target[x, :, lanes] = value
            source, local = target, slice(None)

    @pl.loop(0, rows // 16)
    def _(i):
        both = pl.ds(pl.multiple_of(i * 16, 16), 16)
        start[:HALO] = below_ref[:, both, :].astype(F32)
        start[HALO : HALO + SLAB] = field_ref[:, both, :]
        start[HALO + SLAB :] = above_ref[:, both, :].astype(F32)

        @pl.loop(0, 2)
        def _(k):
            sweep(pl.ds(pl.multiple_of(k * 8, 8), 8))
            at = pl.ds(pl.multiple_of(i * 16 + k * 8, 8), 8)
            out_ref[:, at, :] = even[HALO : HALO + SLAB]

    sums(lambda x: out_ref[x].astype(BF16), core_ref, full_ref, half_ref)


def chebyshev(inside, field, below, above, weight, core_x):
    rows = field.shape[1]
    return call(
        filter_kernel,
        "chebyshev",
        (struct((SLAB, rows, PLANE), F32), struct((rows, NCORE), F32), struct((rows, NCORE), BF16)),
        [pl.BlockSpec(memory_space=pltpu.SMEM)] + [VMEM] * 5,
        [
            pltpu.VMEM((WIDE, 16, PLANE), F32),
            pltpu.VMEM((WIDE, 8, PLANE), F32),
            pltpu.VMEM((WIDE, 8, PLANE), F32),
        ],
    )(inside, field, below, above, weight, core_x)


def clean_kernel(full_ref, a_ref, b_ref, c_ref, field_ref, mapped_ref, core_ref, order_ref, own_ref, density_ref, own, sum_rows):
    coef = total_of(full_ref, a_ref, b_ref, c_ref)
    for x in range(SLAB):
        value = field_ref[x] - dot(coef, core_ref[x])
        own[x * BATCH : (x + 1) * BATCH] = value[:BATCH]
        weighted = jnp.sum(mapped_ref[x].astype(F32) * value, axis=0, keepdims=True)
        sum_rows[x : x + 1] = weighted / (3.0 * BATCH)
    back = row_permutation(BATCH * SLAB, BATCH)
    rest, total = own[...], None
    for _ in range(2):
        part = rest.astype(BF16)
        rest = rest - part.astype(F32)
        moved = dot(dot(back, part).astype(BF16), order_ref[...])
        total = moved if total is None else total + moved
    own_ref[...] = total
    rest, total = sum_rows[...], None
    for _ in range(2):
        part = rest.astype(BF16)
        rest = rest - part.astype(F32)
        moved = dot(part, order_ref[...])
        total = moved if total is None else total + moved
    density_ref[...] = total


def clean(full, others, field, mapped, core_x, order):
    return call(
        clean_kernel,
        "clean",
        (struct((SLAB * BATCH, PLANE), F32), struct((SLAB, PLANE), F32)),
        [VMEM] * 8,
        [pltpu.VMEM((SLAB * BATCH, PLANE), F32), pltpu.VMEM((SLAB, PLANE), F32)],
        limit=12,
    )(full, *others, field, mapped, core_x, order)


def shifted(array, by):
    devices = lax.axis_size("group")
    return lax.ppermute(array, "group", [(i, (i + by) % devices) for i in range(devices)])


def body(stochastic, plane_map, core_orbitals, potential):
    local = potential[0]
    below_v = lax.ppermute(local[SLAB - HALO :], "grid", UP)
    above_v = lax.ppermute(local[:HALO], "grid", DOWN)
    place = lax.axis_index("grid")
    inside = jnp.stack([place > 0, place < GRID - 1]).astype(F32)
    stochastic_later, below_v, above_v, inside = lax.optimization_barrier(
        (stochastic, below_v, above_v, inside)
    )
    third = shifted(stochastic_later, 2)
    second = shifted(stochastic_later, 1)

    order, index_row, weight = prepare(plane_map, local, below_v, above_v)
    core_x = relayout(core_orbitals[0])
    mapped, full, half = map_batches(index_row, core_x, (stochastic, second, third))
    field, low, high = project(full, exchange(half), mapped, core_x)
    below = lax.ppermute(high, "grid", UP)
    above = lax.ppermute(low, "grid", DOWN)
    filtered, full, half = chebyshev(inside, field, below, above, weight, core_x)
    own, density = clean(full, exchange(half), filtered, mapped, core_x, order)
    return density[None], own.reshape(BATCH, SLAB, PLANE)


def solution(mesh):
    return jax.shard_map(
        body,
        mesh=mesh,
        in_specs=(
            P("group", "grid", None),
            P("group", None),
            P("group", None, "grid", None),
            P("group", "grid", None),
        ),
        out_specs=(P("group", "grid", None), P("group", "grid", None)),
        check_vma=False,
    )
```

```python
from fractions import Fraction

import jax
import jax.numpy as jnp
from jax import lax
from jax.experimental import pallas as pl
from jax.experimental.pallas import tpu as pltpu
from jax.sharding import PartitionSpec as P

BZ = 32
KDEG = 6
BATCH = 32
NCORE = 512
SLAB = 8
PLANE = 1024
GRID = 4
HALO = KDEG
WIDE = SLAB + 2 * HALO
LANES = 128
TILES = PLANE // LANES
F32 = jnp.float32
BF16 = jnp.bfloat16


def horner_coefficients():
    cheb = [[Fraction(1)], [Fraction(0), Fraction(1)]]
    for _ in range(2, KDEG + 1):
        last, before = cheb[-1], cheb[-2]
        nxt = [Fraction(0)] + [2 * v for v in last]
        for i, v in enumerate(before):
            nxt[i] -= v
        cheb.append(nxt)
    mono = [Fraction(0)] * (KDEG + 1)
    for k, poly in enumerate(cheb):
        for i, v in enumerate(poly):
            mono[i] += v / (k + 1)
    scaled = [v / Fraction(-8) ** i for i, v in enumerate(mono)]
    top = scaled[KDEG]
    return [float(v / top) for v in scaled], float(top)


EK, TOP = horner_coefficients()

VMEM = pl.BlockSpec(memory_space=pltpu.VMEM)
ANY = pl.BlockSpec(memory_space=pl.ANY)
MIB = 1 << 20
PIECE = 32
CHUNKS = NCORE // PIECE
NT = (((1,), (1,)), ((), ()))


class Line:
    def __init__(self):
        self.token = None

    def call(self, kernel, name, out_shape, args, specs=None, scratch=(), limit=8, micros=2):
        specs = list(specs or [VMEM] * len(args))
        args = list(args)
        waits = self.token is not None
        if waits:
            args.append(self.token)
            specs.append(ANY)
        outs = tuple(out_shape) + (struct((8, LANES), F32),)

        def with_token(*refs):
            ins, rest = refs[: len(args)], refs[len(args) :]
            mine, token, extra = rest[: len(outs) - 1], rest[len(outs) - 1], rest[len(outs) :]
            kernel(*ins[: len(args) - waits], *mine, *extra)
            token[...] = jnp.zeros((8, LANES), F32)

        got = pl.pallas_call(
            with_token,
            in_specs=specs,
            out_specs=tuple(VMEM for _ in outs),
            out_shape=outs,
            scratch_shapes=list(scratch),
            compiler_params=pltpu.CompilerParams(vmem_limit_bytes=limit * MIB),
            cost_estimate=pl.CostEstimate(
                flops=int(micros * 500e6), bytes_accessed=1024, transcendentals=0
            ),
            name=name,
        )(*args)
        self.token = got[-1]
        return got[:-1]


def struct(shape, dtype):
    return jax.ShapeDtypeStruct(shape, dtype)


def one_hot(condition):
    return jnp.where(condition, 1.0, 0.0).astype(BF16)


def iota(shape, axis):
    return lax.broadcasted_iota(jnp.int32, shape, axis)


def dot(a, b):
    return jnp.dot(a, b, preferred_element_type=F32)


def dot_nt(a, b):
    return lax.dot_general(a, b, NT, preferred_element_type=F32)


def split(value, parts):
    out = []
    for _ in range(parts):
        out.append(value.astype(BF16))
        value = value - out[-1].astype(F32)
    return out


def row_permutation(rows, inner):
    outer = rows // inner
    out, src = iota((rows, rows), 0), iota((rows, rows), 1)
    return one_hot(src == (out % outer) * inner + out // outer)


def natural_point(q):
    tile, lane = q // LANES, q % LANES
    return (4 * (lane // 16) + tile // 2) * BZ + 2 * (lane % 16) + tile % 2


def prepare_kernel(index_ref, local_ref, order_ref, pick_ref, local_out):
    order_ref[...] = one_hot(iota((PLANE, PLANE), 1) == natural_point(iota((PLANE, PLANE), 0)))
    index = index_ref[...]
    digits = jnp.concatenate([index // 32, index % 32] + [jnp.zeros((6, PLANE), jnp.int32)], axis=0)
    rows = jnp.concatenate([digits.astype(F32)] + [p.astype(F32) for p in split(local_ref[...], 3)], axis=0)
    moved = dot_nt(rows.astype(BF16), order_ref[...])
    local_out[...] = (moved[8:16] + moved[16:24]) + moved[24:32]
    index = (moved[0:1] * 32.0 + moved[1:2]).astype(jnp.int32)
    pick_ref[...] = one_hot(iota((PLANE, PLANE), 0) == index)


def prepare(line, plane_map, local):
    square = struct((PLANE, PLANE), BF16)
    return line.call(
        prepare_kernel,
        "prepare",
        (square, square, struct((SLAB, PLANE), F32)),
        (plane_map, local),
        micros=2,
    )


def relayout_kernel(core_hbm, out_ref, raw, mids, rows_ref, columns_ref, sems):
    def fetch(i):
        return pltpu.make_async_copy(core_hbm.at[pl.ds(i * 256, 256), :], raw.at[i], sems.at[i])

    for i in range(CHUNKS):
        fetch(i).start()
    rows_ref[...] = row_permutation(256, SLAB)
    src, out = iota((256, 256), 0), iota((256, 256), 1)
    piece, low = out // PIECE, out % PIECE
    columns_ref[...] = one_hot(src == (4 * (low // 16) + piece // 2) * BZ + 2 * (low % 16) + piece % 2)
    lane = iota((PIECE, LANES), 1)
    half, quarter = lane < 64, lane % 64 < 32

    def permute(i, mid):
        for b in range(4):
            cols = pl.ds(b * 256, 256)
            ordered = dot(rows_ref[...], raw[i, :, cols]).astype(BF16)
            mid[:, cols] = dot(ordered, columns_ref[...]).astype(BF16)

    def gather(i, mid):
        at = pl.ds(pl.multiple_of(i * PIECE, PIECE), PIECE)
        for x in range(SLAB):
            for h in range(2):
                p = [
                    mid[pl.ds(x * PIECE, PIECE), pl.ds(b * 256 + h * LANES, LANES)]
                    for b in range(4)
                ]
                u = [jnp.where(half, p[k], pltpu.roll(p[k + 2], 64, 1)) for k in range(2)]
                v = [jnp.where(half, pltpu.roll(p[k], 64, 1), p[k + 2]) for k in range(2)]
                for k, (a, c) in enumerate((u, v)):
                    j = 4 * h + 2 * k
                    out_ref[x, at, pl.ds(j * LANES, LANES)] = jnp.where(
                        quarter, a, pltpu.roll(c, 32, 1)
                    )
                    out_ref[x, at, pl.ds((j + 1) * LANES, LANES)] = jnp.where(
                        quarter, pltpu.roll(a, LANES - 32, 1), c
                    )

    @pl.loop(0, CHUNKS // 4)
    def _(i):
        for k in range(4):
            fetch(4 * i + k).wait()
        for k in range(5):
            if k < 4:
                permute(4 * i + k, mids.at[k])
            if k > 0:
                gather(4 * i + k - 1, mids.at[k - 1])


def relayout(line, core):
    square = pltpu.VMEM((256, 256), BF16)
    return line.call(
        relayout_kernel,
        "relayout",
        (struct((SLAB, NCORE, PLANE), BF16),),
        (core.reshape(NCORE * SLAB, PLANE),),
        specs=[pl.BlockSpec(memory_space=pltpu.HBM)],
        scratch=[
            pltpu.VMEM((CHUNKS, 256, PLANE), BF16),
            pltpu.VMEM((4, 256, PLANE), BF16),
            square,
            square,
            pltpu.SemaphoreType.DMA((CHUNKS,)),
        ],
        limit=42,
        micros=8,
    )[0]


def sums(field_of, core_ref, full_ref, half_ref):
    for x in range(SLAB):
        part = dot_nt(field_of(x), core_ref[x])
        if x == 0:
            full_ref[...] = part
        else:
            full_ref[...] += part
    half_ref[...] = full_ref[...].astype(BF16)


def map_kernel(counts, pick_ref, core_ref, *refs):
    sources, (out_ref, full_ref, half_ref) = refs[:-3], refs[-3:]
    perm = row_permutation(BATCH * SLAB, SLAB)
    for b, count in enumerate(counts):
        value = sources[0][...]
        if count == 2:
            value = value + sources[1][...]
        sources = sources[count:]
        got = dot(dot(perm, value).astype(BF16), pick_ref[...]).astype(BF16)
        out_ref[:, b * BATCH : (b + 1) * BATCH, :] = got.reshape(SLAB, BATCH, PLANE)
    sums(lambda x: out_ref[x], core_ref, full_ref, half_ref)


def map_batches(line, pick, core_x, batches):
    rows = BATCH * len(batches)
    counts = tuple(len(b) for b in batches)
    flat = [a.reshape(BATCH * SLAB, PLANE) for b in batches for a in b]
    return line.call(
        lambda *refs: map_kernel(counts, *refs),
        "map_batches",
        (struct((SLAB, rows, PLANE), BF16), struct((rows, NCORE), F32), struct((rows, NCORE), BF16)),
        (pick, core_x, *flat),
        micros=2 + len(batches) // 2,
    )


def exchange(half):
    return [
        lax.ppermute(half, "grid", [(i, i ^ k) for i in range(GRID)]) for k in range(1, GRID)
    ]


def total_of(full_ref, a_ref, b_ref, c_ref):
    rest = a_ref[...].astype(F32) + b_ref[...].astype(F32) + c_ref[...].astype(F32)
    return (full_ref[...] + rest).astype(BF16)


def project_kernel(full_ref, a_ref, b_ref, c_ref, field_ref, core_ref, *refs):
    local_ref = refs[0] if len(refs) == 4 else None
    out_ref, low_ref, high_ref = refs[-3:]
    rows = field_ref.shape[1]
    coef = total_of(full_ref, a_ref, b_ref, c_ref)
    for x in range(SLAB):
        value = field_ref[x].astype(F32) - dot(coef, core_ref[x])
        out_ref[x] = value
        short = value.astype(BF16)
        if local_ref is not None:
            parts = [p.astype(F32) for p in split(local_ref[x : x + 1], 3)]
            rest = jnp.zeros((12, PLANE), F32)
            extra = jnp.concatenate(parts + [jnp.ones((1, PLANE), F32), rest], axis=0)
            short = jnp.concatenate([short, extra.astype(BF16)], axis=0)
        if x < HALO:
            low_ref[x] = short
        if x >= SLAB - HALO:
            high_ref[x - (SLAB - HALO)] = short


def project(line, full, others, field, core_x, local):
    rows = field.shape[1]
    sent = rows + (16 if local is not None else 0)
    return line.call(
        project_kernel,
        "project",
        (
            struct((SLAB, rows, PLANE), F32),
            struct((HALO, sent, PLANE), BF16),
            struct((HALO, sent, PLANE), BF16),
        ),
        (full, *others, field, core_x) + ((local,) if local is not None else ()),
        micros=2,
    )


UP = [(i, i + 1) for i in range(GRID - 1)]
DOWN = [(j, i) for i, j in UP]


def filter_kernel(given, *refs):
    field_ref, below_ref, above_ref, core_ref = refs[:4]
    if given:
        weight_ref, flag_ref, out_ref, full_ref, half_ref = refs[4:9]
    else:
        local_ref, weight_ref, flag_ref, out_ref, full_ref, half_ref = refs[4:10]
    below, above, even, odd = refs[-4:]
    rows = field_ref.shape[1]
    if not given:
        weight_ref[HALO : HALO + SLAB] = 8.0 * local_ref[...] - 2.0
        for k, ref in enumerate((below_ref, above_ref)):
            for x in range(HALO):
                extra = ref[x, rows : rows + 16, :].astype(F32)
                near = (extra[0:1] + extra[1:2]) + extra[2:3]
                place = x if k == 0 else HALO + SLAB + x
                weight_ref[place : place + 1] = 8.0 * near - 2.0
                if x == 0:
                    flag_ref[k] = jnp.broadcast_to(extra[3:4, :LANES], (8, LANES))
    lane = iota((8, LANES), 1)
    head, tail = lane < 16, lane >= LANES - 16
    first_z, last_z = lane % 16 == 0, lane % 16 == 15
    low_flag, high_flag = flag_ref[0], flag_ref[1]

    def rolled(mask, value, by):
        return pltpu.roll(jnp.where(mask, 0.0, value), by % LANES, 1)

    def sweep(local, at):
        def begin(x, lanes):
            if x < HALO:
                return below[x, local, lanes]
            if x >= HALO + SLAB:
                return above[x - HALO - SLAB, local, lanes]
            return field_ref[x - HALO, at, lanes]

        def tiles(source, x):
            every = [pl.ds(j * LANES, LANES) for j in range(TILES)]
            if source is None:
                return [begin(x, lanes) for lanes in every]
            return [source[x, :, lanes] for lanes in every]

        source = None
        for k in range(1, KDEG + 1):
            target = even if k % 2 == 0 else odd
            first, last = k, WIDE - k
            here, after = tiles(source, first - 1), tiles(source, first)
            for x in range(first, last):
                before, here = here, after
                after = tiles(source, x + 1)
                up = [rolled(head, here[j], -16) for j in range(2)]
                down = [rolled(tail, here[j], 16) for j in range(6, 8)]
                for j in range(TILES):
                    lanes = pl.ds(j * LANES, LANES)
                    c = here[j]
                    above_y = here[j + 2] if j < 6 else up[j - 6]
                    below_y = here[j - 2] if j > 1 else down[j]
                    mate = here[j ^ 1]
                    z = mate + (rolled(first_z, mate, -1) if j % 2 else rolled(last_z, mate, 1))
                    around = (before[j] + after[j]) + (above_y + below_y) + z
                    w = jnp.broadcast_to(weight_ref[pl.ds(x, 1), lanes], (8, LANES))
                    value = around - w * c + EK[KDEG - k] * begin(x, lanes)
                    if x == HALO - 1:
                        value = value * low_flag
                    elif x == HALO + SLAB:
                        value = value * high_flag
                    if k == KDEG:
                        out_ref[x - HALO, at, lanes] = value * TOP
                    else:
                        target[x, :, lanes] = value
            source = target

    @pl.loop(0, rows // 16)
    def _(i):
        both = pl.ds(pl.multiple_of(i * 16, 16), 16)
        below[...] = below_ref[:, both, :].astype(F32)
        above[...] = above_ref[:, both, :].astype(F32)

        @pl.loop(0, 2)
        def _(k):
            sweep(
                pl.ds(pl.multiple_of(k * 8, 8), 8),
                pl.ds(pl.multiple_of(i * 16 + k * 8, 8), 8),
            )

    sums(lambda x: out_ref[x].astype(BF16), core_ref, full_ref, half_ref)


def chebyshev(line, field, below, above, core_x, local, weight):
    rows = field.shape[1]
    made = (struct((WIDE, PLANE), F32), struct((2, 8, LANES), F32))
    given = weight is not None
    got = line.call(
        lambda *refs: filter_kernel(given, *refs),
        "chebyshev",
        (() if given else made)
        + (struct((SLAB, rows, PLANE), F32), struct((rows, NCORE), F32), struct((rows, NCORE), BF16)),
        (field, below, above, core_x) + (tuple(weight) if given else (local,)),
        scratch=[
            pltpu.VMEM((HALO, 16, PLANE), F32),
            pltpu.VMEM((HALO, 16, PLANE), F32),
            pltpu.VMEM((WIDE, 8, PLANE), F32),
            pltpu.VMEM((WIDE, 8, PLANE), F32),
        ],
        micros=2 + rows // 5,
    )
    return (weight, got) if given else (got[:2], got[2:])


def reorder(value, order_ref):
    parts = split(value, 2)
    return dot(parts[0], order_ref[...]) + dot(parts[1], order_ref[...])


def clean_kernel(first, last, *refs):
    refs = list(refs)
    full_ref, a_ref, b_ref, c_ref, field_ref, mapped_ref, core_ref = refs[:7]
    refs = refs[7:]
    order_ref = refs.pop(0) if first or last else None
    before_ref = None if first else refs.pop(0)
    own_ref = refs.pop(0) if first else None
    density_ref = refs.pop(0)
    own = refs.pop(0) if first else None
    rows = refs.pop(0)
    coef = total_of(full_ref, a_ref, b_ref, c_ref)
    for x in range(SLAB):
        value = field_ref[x] - dot(coef, core_ref[x])
        if first:
            own[x * BATCH : (x + 1) * BATCH] = value[:BATCH]
        weighted = jnp.sum(mapped_ref[x].astype(F32) * value, axis=0, keepdims=True)
        rows[x : x + 1] = weighted / (3.0 * BATCH)
    if first:
        back = row_permutation(BATCH * SLAB, BATCH)
        total = None
        for part in split(own[...], 2):
            moved = dot(dot(back, part).astype(BF16), order_ref[...])
            total = moved if total is None else total + moved
        own_ref[...] = total
    density = rows[...] if first else rows[...] + before_ref[...]
    density_ref[...] = reorder(density, order_ref) if last else density


def clean(line, full, others, field, mapped, core_x, order, density, first, last):
    args = [full, *others, field, mapped, core_x]
    if first or last:
        args.append(order)
    if not first:
        args.append(density)
    small = struct((SLAB, PLANE), F32)
    own = struct((SLAB * BATCH, PLANE), F32)
    got = line.call(
        lambda *refs: clean_kernel(first, last, *refs),
        "clean",
        (own, small) if first else (small,),
        args,
        scratch=([pltpu.VMEM(own.shape, F32)] if first else []) + [pltpu.VMEM(small.shape, F32)],
        limit=12,
        micros=3,
    )
    return (got[0], got[1]) if first else (None, got[0])


def permute_groups(array, pairs):
    return lax.ppermute(array, "group", pairs)


def body(stochastic, plane_map, core_orbitals, potential):
    groups = lax.axis_size("group")
    third = permute_groups(stochastic, [(i, (i + 2) % groups) for i in range(groups)])
    to_odd = permute_groups(stochastic, [(i, i + 1) for i in range(0, groups, 2)])
    to_even = None

    line = Line()
    core_x = relayout(line, core_orbitals[0])
    order, pick, local = prepare(line, plane_map, potential[0])
    state = {}
    weight = density = own = None
    for step, c in PLAN:
        s = state.setdefault(c, {})
        if step == "forward":
            third, line.token = lax.optimization_barrier((third, line.token))
            to_even = permute_groups(third, [(i + 1, i) for i in range(0, groups, 2)])
        elif step == "map":
            batches = [(stochastic,), (to_odd, to_even), (third,)]
            visits = [batches[t] for t in VISITS[c]]
            s["mapped"], s["full"], half = map_batches(line, pick, core_x, visits)
            s["others"] = exchange(half)
        elif step == "project":
            s["field"], low, high = project(
                line, s["full"], s["others"], s["mapped"], core_x, local if c == 0 else None
            )
            s["below"] = lax.ppermute(high, "grid", UP)
            s["above"] = lax.ppermute(low, "grid", DOWN)
        elif step == "filter":
            weight, (s["done"], s["full"], half) = chebyshev(
                line, s["field"], s["below"], s["above"], core_x, local, weight
            )
            s["others"] = exchange(half)
        elif step == "clean":
            got, density = clean(
                line, s["full"], s["others"], s["done"], s["mapped"], core_x, order, density,
                c == 0, c == len(VISITS) - 1,
            )
            own = got if c == 0 else own
    return density[None], own.reshape(BATCH, SLAB, PLANE)


VISITS = ((0,), (2, 1))
PLAN = (
    ("map", 0),
    ("forward", 0),
    ("project", 0),
    ("map", 1),
    ("project", 1),
    ("filter", 0),
    ("filter", 1),
    ("clean", 0),
    ("clean", 1),
)


def solution(mesh):
    return jax.shard_map(
        body,
        mesh=mesh,
        in_specs=(
            P("group", "grid", None),
            P("group", None),
            P("group", None, "grid", None),
            P("group", "grid", None),
        ),
        out_specs=(P("group", "grid", None), P("group", "grid", None)),
        check_vma=False,
    )
```

```python
from fractions import Fraction

import jax
import jax.numpy as jnp
from jax import lax
from jax.experimental import pallas as pl
from jax.experimental.pallas import tpu as pltpu
from jax.sharding import PartitionSpec as P

BZ = 32
KDEG = 6
BATCH = 32
NCORE = 512
SLAB = 8
PLANE = 1024
GRID = 4
HALO = KDEG
WIDE = SLAB + 2 * HALO
LANES = 128
TILES = PLANE // LANES
F32 = jnp.float32
BF16 = jnp.bfloat16


def horner_coefficients():
    cheb = [[Fraction(1)], [Fraction(0), Fraction(1)]]
    for _ in range(2, KDEG + 1):
        last, before = cheb[-1], cheb[-2]
        nxt = [Fraction(0)] + [2 * v for v in last]
        for i, v in enumerate(before):
            nxt[i] -= v
        cheb.append(nxt)
    mono = [Fraction(0)] * (KDEG + 1)
    for k, poly in enumerate(cheb):
        for i, v in enumerate(poly):
            mono[i] += v / (k + 1)
    scaled = [v / Fraction(-8) ** i for i, v in enumerate(mono)]
    top = scaled[KDEG]
    return [float(v / top) for v in scaled], float(top)


EK, TOP = horner_coefficients()

VMEM = pl.BlockSpec(memory_space=pltpu.VMEM)
ANY = pl.BlockSpec(memory_space=pl.ANY)
MIB = 1 << 20
PIECE = 32
CHUNKS = NCORE // PIECE
NT = (((1,), (1,)), ((), ()))


class Line:
    def __init__(self):
        self.token = None

    def call(self, kernel, name, out_shape, args, specs=None, scratch=(), limit=8, micros=2):
        specs = list(specs or [VMEM] * len(args))
        args = list(args)
        waits = self.token is not None
        if waits:
            args.append(self.token)
            specs.append(ANY)
        outs = tuple(out_shape) + (struct((8, LANES), F32),)

        def with_token(*refs):
            ins, rest = refs[: len(args)], refs[len(args) :]
            mine, token, extra = rest[: len(outs) - 1], rest[len(outs) - 1], rest[len(outs) :]
            kernel(*ins[: len(args) - waits], *mine, *extra)
            token[...] = jnp.zeros((8, LANES), F32)

        got = pl.pallas_call(
            with_token,
            in_specs=specs,
            out_specs=tuple(VMEM for _ in outs),
            out_shape=outs,
            scratch_shapes=list(scratch),
            compiler_params=pltpu.CompilerParams(vmem_limit_bytes=limit * MIB),
            cost_estimate=pl.CostEstimate(
                flops=int(micros * 500e6), bytes_accessed=1024, transcendentals=0
            ),
            name=name,
        )(*args)
        self.token = got[-1]
        return got[:-1]


def struct(shape, dtype):
    return jax.ShapeDtypeStruct(shape, dtype)


def one_hot(condition):
    return jnp.where(condition, 1.0, 0.0).astype(BF16)


def iota(shape, axis):
    return lax.broadcasted_iota(jnp.int32, shape, axis)


def dot(a, b):
    return jnp.dot(a, b, preferred_element_type=F32)


def dot_nt(a, b):
    return lax.dot_general(a, b, NT, preferred_element_type=F32)


def split(value, parts):
    out = []
    for _ in range(parts):
        out.append(value.astype(BF16))
        value = value - out[-1].astype(F32)
    return out


def row_permutation(rows, inner):
    outer = rows // inner
    out, src = iota((rows, rows), 0), iota((rows, rows), 1)
    return one_hot(src == (out % outer) * inner + out // outer)


def natural_point(q):
    tile, lane = q // LANES, q % LANES
    return (4 * (lane // 16) + tile // 2) * BZ + 2 * (lane % 16) + tile % 2


def prepare_kernel(index_ref, local_ref, order_ref, pick_ref, local_out):
    order_ref[...] = one_hot(iota((PLANE, PLANE), 1) == natural_point(iota((PLANE, PLANE), 0)))
    index = index_ref[...]
    digits = jnp.concatenate([index // 32, index % 32] + [jnp.zeros((6, PLANE), jnp.int32)], axis=0)
    rows = jnp.concatenate([digits.astype(F32)] + [p.astype(F32) for p in split(local_ref[...], 3)], axis=0)
    moved = dot_nt(rows.astype(BF16), order_ref[...])
    local_out[...] = (moved[8:16] + moved[16:24]) + moved[24:32]
    index = (moved[0:1] * 32.0 + moved[1:2]).astype(jnp.int32)
    pick_ref[...] = one_hot(iota((PLANE, PLANE), 0) == index)


def prepare(line, plane_map, local):
    square = struct((PLANE, PLANE), BF16)
    return line.call(
        prepare_kernel,
        "prepare",
        (square, square, struct((SLAB, PLANE), F32)),
        (plane_map, local),
        micros=2,
    )


def relayout_kernel(core_hbm, out_ref, raw, mids, rows_ref, columns_ref, sems):
    def fetch(i):
        return pltpu.make_async_copy(core_hbm.at[pl.ds(i * 256, 256), :], raw.at[i], sems.at[i])

    for i in range(CHUNKS):
        fetch(i).start()
    rows_ref[...] = row_permutation(256, SLAB)
    src, out = iota((256, 256), 0), iota((256, 256), 1)
    piece, low = out // PIECE, out % PIECE
    columns_ref[...] = one_hot(src == (4 * (low // 16) + piece // 2) * BZ + 2 * (low % 16) + piece % 2)
    lane = iota((PIECE, LANES), 1)
    half, quarter = lane < 64, lane % 64 < 32

    def permute(i, mid):
        for b in range(4):
            cols = pl.ds(b * 256, 256)
            ordered = dot(rows_ref[...], raw[i, :, cols]).astype(BF16)
            mid[:, cols] = dot(ordered, columns_ref[...]).astype(BF16)

    def gather(i, mid):
        at = pl.ds(pl.multiple_of(i * PIECE, PIECE), PIECE)
        for x in range(SLAB):
            for h in range(2):
                p = [
                    mid[pl.ds(x * PIECE, PIECE), pl.ds(b * 256 + h * LANES, LANES)]
                    for b in range(4)
                ]
                u = [jnp.where(half, p[k], pltpu.roll(p[k + 2], 64, 1)) for k in range(2)]
                v = [jnp.where(half, pltpu.roll(p[k], 64, 1), p[k + 2]) for k in range(2)]
                for k, (a, c) in enumerate((u, v)):
                    j = 4 * h + 2 * k
                    out_ref[x, at, pl.ds(j * LANES, LANES)] = jnp.where(
                        quarter, a, pltpu.roll(c, 32, 1)
                    )
                    out_ref[x, at, pl.ds((j + 1) * LANES, LANES)] = jnp.where(
                        quarter, pltpu.roll(a, LANES - 32, 1), c
                    )

    @pl.loop(0, CHUNKS // 4)
    def _(i):
        for k in range(4):
            fetch(4 * i + k).wait()
        for k in range(5):
            if k < 4:
                permute(4 * i + k, mids.at[k])
            if k > 0:
                gather(4 * i + k - 1, mids.at[k - 1])


def relayout(line, core):
    square = pltpu.VMEM((256, 256), BF16)
    return line.call(
        relayout_kernel,
        "relayout",
        (struct((SLAB, NCORE, PLANE), BF16),),
        (core.reshape(NCORE * SLAB, PLANE),),
        specs=[pl.BlockSpec(memory_space=pltpu.HBM)],
        scratch=[
            pltpu.VMEM((CHUNKS, 256, PLANE), BF16),
            pltpu.VMEM((4, 256, PLANE), BF16),
            square,
            square,
            pltpu.SemaphoreType.DMA((CHUNKS,)),
        ],
        limit=42,
        micros=8,
    )[0]


def sums(field_of, core_ref, full_ref, half_ref):
    for x in range(SLAB):
        part = dot_nt(field_of(x), core_ref[x])
        if x == 0:
            full_ref[...] = part
        else:
            full_ref[...] += part
    half_ref[...] = full_ref[...].astype(BF16)


def map_kernel(counts, pick_ref, core_ref, *refs):
    sources, (out_ref, full_ref, half_ref) = refs[:-3], refs[-3:]
    perm = row_permutation(BATCH * SLAB, SLAB)
    for b, count in enumerate(counts):
        value = sources[0][...]
        if count == 2:
            odd = lax.axis_index("group") % 2 == 1
            value = jnp.where(odd, value, sources[1][...])
        sources = sources[count:]
        got = dot(dot(perm, value).astype(BF16), pick_ref[...]).astype(BF16)
        out_ref[:, b * BATCH : (b + 1) * BATCH, :] = got.reshape(SLAB, BATCH, PLANE)
    sums(lambda x: out_ref[x], core_ref, full_ref, half_ref)


def map_batches(line, pick, core_x, batches):
    rows = BATCH * len(batches)
    counts = tuple(len(b) for b in batches)
    flat = [a.reshape(BATCH * SLAB, PLANE) for b in batches for a in b]
    return line.call(
        lambda *refs: map_kernel(counts, *refs),
        "map_batches",
        (struct((SLAB, rows, PLANE), BF16), struct((rows, NCORE), F32), struct((rows, NCORE), BF16)),
        (pick, core_x, *flat),
        micros=2 + len(batches) // 2,
    )


def exchange(half):
    return [
        lax.ppermute(half, "grid", [(i, i ^ k) for i in range(GRID)]) for k in range(1, GRID)
    ]


def total_of(full_ref, a_ref, b_ref, c_ref):
    rest = a_ref[...].astype(F32) + b_ref[...].astype(F32) + c_ref[...].astype(F32)
    return (full_ref[...] + rest).astype(BF16)


def project_kernel(full_ref, a_ref, b_ref, c_ref, field_ref, core_ref, *refs):
    local_ref = refs[0] if len(refs) == 4 else None
    out_ref, low_ref, high_ref = refs[-3:]
    rows = field_ref.shape[1]
    coef = total_of(full_ref, a_ref, b_ref, c_ref)
    for x in range(SLAB):
        value = field_ref[x].astype(F32) - dot(coef, core_ref[x])
        out_ref[x] = value
        short = value.astype(BF16)
        if local_ref is not None:
            parts = [p.astype(F32) for p in split(local_ref[x : x + 1], 3)]
            rest = jnp.zeros((12, PLANE), F32)
            extra = jnp.concatenate(parts + [jnp.ones((1, PLANE), F32), rest], axis=0)
            short = jnp.concatenate([short, extra.astype(BF16)], axis=0)
        if x < HALO:
            low_ref[x] = short
        if x >= SLAB - HALO:
            high_ref[x - (SLAB - HALO)] = short


def project(line, full, others, field, core_x, local):
    rows = field.shape[1]
    sent = rows + (16 if local is not None else 0)
    return line.call(
        project_kernel,
        "project",
        (
            struct((SLAB, rows, PLANE), F32),
            struct((HALO, sent, PLANE), BF16),
            struct((HALO, sent, PLANE), BF16),
        ),
        (full, *others, field, core_x) + ((local,) if local is not None else ()),
        micros=2,
    )


UP = [(i, i + 1) for i in range(GRID - 1)]
DOWN = [(j, i) for i, j in UP]


def filter_kernel(ahead, *refs):
    field_ref, below_ref, above_ref = refs[:3]
    if ahead:
        local_ref, weight_ref, first_ref, flag_ref, out_ref = refs[3:8]
    else:
        weight_ref, first_ref, flag_ref, core_ref, other_ref, out_ref, full_ref, half_ref = refs[3:11]
    below, above, even, odd = refs[-4:]
    rows = field_ref.shape[1]
    if ahead:
        weight_ref[HALO : HALO + SLAB] = 8.0 * local_ref[...] - 2.0
        for k, ref in enumerate((below_ref, above_ref)):
            for x in range(HALO):
                extra = ref[x, rows : rows + 16, :].astype(F32)
                near = (extra[0:1] + extra[1:2]) + extra[2:3]
                place = x if k == 0 else HALO + SLAB + x
                weight_ref[place : place + 1] = 8.0 * near - 2.0
                if x == 0:
                    flag_ref[k] = jnp.broadcast_to(extra[3:4, :LANES], (8, LANES))
        first_ref[...] = weight_ref[...] - EK[KDEG - 1]
    lane = iota((8, LANES), 1)
    head, tail = lane < 16, lane >= LANES - 16
    first_z, last_z = lane % 16 == 0, lane % 16 == 15
    low_flag, high_flag = flag_ref[0], flag_ref[1]

    def rolled(mask, value, by):
        return pltpu.roll(jnp.where(mask, 0.0, value), by % LANES, 1)

    def sweep(local, at):
        def begin(x, lanes):
            if x < HALO:
                return below[x, local, lanes]
            if x >= HALO + SLAB:
                return above[x - HALO - SLAB, local, lanes]
            return field_ref[x - HALO, at, lanes]

        def tiles(source, x):
            every = [pl.ds(j * LANES, LANES) for j in range(TILES)]
            if source is None:
                return [begin(x, lanes) for lanes in every]
            return [source[x, :, lanes] for lanes in every]

        source = None
        for k in range(1, KDEG + 1):
            target = even if k % 2 == 0 else odd
            first, last = k, WIDE - k
            here, after = tiles(source, first - 1), tiles(source, first)
            for x in range(first, last):
                before, here = here, after
                after = tiles(source, x + 1)
                up = [rolled(head, here[j], -16) for j in range(2)]
                down = [rolled(tail, here[j], 16) for j in range(6, 8)]
                for j in range(TILES):
                    lanes = pl.ds(j * LANES, LANES)
                    c = here[j]
                    above_y = here[j + 2] if j < 6 else up[j - 6]
                    below_y = here[j - 2] if j > 1 else down[j]
                    mate = here[j ^ 1]
                    z = mate + (rolled(first_z, mate, -1) if j % 2 else rolled(last_z, mate, 1))
                    around = (before[j] + after[j]) + (above_y + below_y) + z
                    w_ref = first_ref if k == 1 else weight_ref
                    w = jnp.broadcast_to(w_ref[pl.ds(x, 1), lanes], (8, LANES))
                    value = around - w * c
                    if k > 1:
                        value = value + EK[KDEG - k] * begin(x, lanes)
                    if x == HALO - 1:
                        value = value * low_flag
                    elif x == HALO + SLAB:
                        value = value * high_flag
                    if k == KDEG:
                        out_ref[x - HALO, at, lanes] = value * TOP
                    else:
                        target[x, :, lanes] = value
            source = target

    @pl.loop(0, rows // 16)
    def _(i):
        both = pl.ds(pl.multiple_of(i * 16, 16), 16)
        below[...] = below_ref[:, both, :].astype(F32)
        above[...] = above_ref[:, both, :].astype(F32)

        @pl.loop(0, 2)
        def _(k):
            sweep(
                pl.ds(pl.multiple_of(k * 8, 8), 8),
                pl.ds(pl.multiple_of(i * 16 + k * 8, 8), 8),
            )

    if not ahead:

        def both_of(x):
            return jnp.concatenate([other_ref[x].astype(BF16), out_ref[x].astype(BF16)], axis=0)

        sums(both_of, core_ref, full_ref, half_ref)


def filter_scratch():
    halo, whole = pltpu.VMEM((HALO, 16, PLANE), F32), pltpu.VMEM((WIDE, 8, PLANE), F32)
    return [halo, halo, whole, whole]


def filter_ahead(line, field, below, above, local):
    rows = field.shape[1]
    wide = struct((WIDE, PLANE), F32)
    got = line.call(
        lambda *refs: filter_kernel(True, *refs),
        "filter_ahead",
        (wide, wide, struct((2, 8, LANES), F32), struct((SLAB, rows, PLANE), F32)),
        (field, below, above, local),
        scratch=filter_scratch(),
        micros=7,
    )
    return got[:3], got[3]


def filter_rest(line, field, below, above, weight, core_x, ahead):
    rows = field.shape[1]
    total = rows + ahead.shape[1]
    return line.call(
        lambda *refs: filter_kernel(False, *refs),
        "filter_rest",
        (struct((SLAB, rows, PLANE), F32), struct((total, NCORE), F32), struct((total, NCORE), BF16)),
        (field, below, above, *weight, core_x, ahead),
        scratch=filter_scratch(),
        micros=14,
    )


def reorder(value, order_ref):
    parts = split(value, 2)
    return dot(parts[0], order_ref[...]) + dot(parts[1], order_ref[...])


def clean_kernel(full_ref, a_ref, b_ref, c_ref, ahead_ref, rest_ref, mapped_ref, mapped_rest_ref, core_ref, order_ref, own_ref, density_ref, own, rows):
    coef = total_of(full_ref, a_ref, b_ref, c_ref)
    for x in range(SLAB):
        taken = dot(coef, core_ref[x])
        ahead = ahead_ref[x] - taken[:BATCH]
        rest = rest_ref[x] - taken[BATCH:]
        own[x * BATCH : (x + 1) * BATCH] = ahead
        weighted = jnp.sum(mapped_ref[x].astype(F32) * ahead, axis=0, keepdims=True)
        weighted += jnp.sum(mapped_rest_ref[x].astype(F32) * rest, axis=0, keepdims=True)
        rows[x : x + 1] = weighted / (3.0 * BATCH)
    back = row_permutation(BATCH * SLAB, BATCH)
    total = None
    for part in split(own[...], 2):
        moved = dot(dot(back, part).astype(BF16), order_ref[...])
        total = moved if total is None else total + moved
    own_ref[...] = total
    density_ref[...] = reorder(rows[...], order_ref)


def clean(line, full, others, ahead, rest, mapped, mapped_rest, core_x, order):
    small, own = struct((SLAB, PLANE), F32), struct((SLAB * BATCH, PLANE), F32)
    return line.call(
        clean_kernel,
        "clean",
        (own, small),
        (full, *others, ahead, rest, mapped, mapped_rest, core_x, order),
        scratch=[pltpu.VMEM(own.shape, F32), pltpu.VMEM(small.shape, F32)],
        limit=12,
        micros=4,
    )


def permute_groups(array, pairs):
    return lax.ppermute(array, "group", pairs)


def body(stochastic, plane_map, core_orbitals, potential):
    groups = lax.axis_size("group")
    mate = permute_groups(stochastic, [(i, i ^ 1) for i in range(groups)])
    third = permute_groups(stochastic, [(i, (i + 2) % groups) for i in range(groups)])

    line = Line()
    core_x = relayout(line, core_orbitals[0])
    order, pick, local = prepare(line, plane_map, potential[0])

    mapped, full, half = map_batches(line, pick, core_x, [(stochastic,)])
    others = exchange(half)
    mate, line.token = lax.optimization_barrier((mate, line.token))
    second = permute_groups(mate, [(i, (i + 2) % groups) for i in range(0, groups, 2)])
    field, low, high = project(line, full, others, mapped, core_x, local)
    below, above = lax.ppermute(high, "grid", UP), lax.ppermute(low, "grid", DOWN)

    mapped_rest, full, half = map_batches(line, pick, core_x, [(third,), (mate, second)])
    rest, low, high = project(line, full, exchange(half), mapped_rest, core_x, None)
    below_rest, above_rest = lax.ppermute(high, "grid", UP), lax.ppermute(low, "grid", DOWN)

    weight, ahead = filter_ahead(line, field, below, above, local)
    rest, full, half = filter_rest(line, rest, below_rest, above_rest, weight, core_x, ahead)
    own, density = clean(
        line, full, exchange(half), ahead, rest, mapped, mapped_rest, core_x, order
    )
    return density[None], own.reshape(BATCH, SLAB, PLANE)


def solution(mesh):
    return jax.shard_map(
        body,
        mesh=mesh,
        in_specs=(
            P("group", "grid", None),
            P("group", None),
            P("group", None, "grid", None),
            P("group", "grid", None),
        ),
        out_specs=(P("group", "grid", None), P("group", "grid", None)),
        check_vma=False,
    )
```

```python
from fractions import Fraction

import jax
import jax.numpy as jnp
from jax import lax
from jax.experimental import pallas as pl
from jax.experimental.pallas import tpu as pltpu
from jax.sharding import PartitionSpec as P


BZ = 32
KDEG = 6
BATCH = 32
NCORE = 512
SLAB = 8
PLANE = 1024
GRID = 4
HALO = KDEG
WIDE = SLAB + 2 * HALO
LANES = 128
TILES = PLANE // LANES
F32 = jnp.float32
BF16 = jnp.bfloat16


def horner_coefficients():
    cheb = [[Fraction(1)], [Fraction(0), Fraction(1)]]
    for _ in range(2, KDEG + 1):
        last, before = cheb[-1], cheb[-2]
        nxt = [Fraction(0)] + [2 * v for v in last]
        for i, v in enumerate(before):
            nxt[i] -= v
        cheb.append(nxt)
    mono = [Fraction(0)] * (KDEG + 1)
    for k, poly in enumerate(cheb):
        for i, v in enumerate(poly):
            mono[i] += v / (k + 1)
    scaled = [v / Fraction(-8) ** i for i, v in enumerate(mono)]
    top = scaled[KDEG]
    return [float(v / top) for v in scaled], float(top)


EK, TOP = horner_coefficients()

VMEM = pl.BlockSpec(memory_space=pltpu.VMEM)
ANY = pl.BlockSpec(memory_space=pl.ANY)
MIB = 1 << 20
PIECE = 32
SCALE = 500e6
CHUNKS = NCORE // PIECE
NT = (((1,), (1,)), ((), ()))


class Line:
    def __init__(self):
        self.token = None

    def call(self, kernel, out_shape, args, specs=None, scratch=(), limit=8, micros=2):
        specs = list(specs or [VMEM] * len(args))
        args = list(args)
        waits = self.token is not None
        if waits:
            args.append(self.token)
            specs.append(ANY)
        outs = tuple(out_shape) + (struct((8, LANES), F32),)

        def with_token(*refs):
            ins, rest = refs[: len(args)], refs[len(args) :]
            mine, token, extra = rest[: len(outs) - 1], rest[len(outs) - 1], rest[len(outs) :]
            kernel(*ins[: len(args) - waits], *mine, *extra)
            token[...] = jnp.zeros((8, LANES), F32)

        got = pl.pallas_call(
            with_token,
            in_specs=specs,
            out_specs=tuple(VMEM for _ in outs),
            out_shape=outs,
            scratch_shapes=list(scratch),
            compiler_params=pltpu.CompilerParams(vmem_limit_bytes=limit * MIB),
            cost_estimate=pl.CostEstimate(
                flops=int(micros * SCALE), bytes_accessed=1024, transcendentals=0
            ),
        )(*args)
        self.token = got[-1]
        return got[:-1]


def struct(shape, dtype):
    return jax.ShapeDtypeStruct(shape, dtype)


def one_hot(condition):
    return jnp.where(condition, 1.0, 0.0).astype(BF16)


def iota(shape, axis):
    return lax.broadcasted_iota(jnp.int32, shape, axis)


def dot(a, b):
    return jnp.dot(a, b, preferred_element_type=F32)


def dot_nt(a, b):
    return lax.dot_general(a, b, NT, preferred_element_type=F32)


def split(value, parts):
    out = []
    for _ in range(parts):
        out.append(value.astype(BF16))
        value = value - out[-1].astype(F32)
    return out


def row_permutation(rows, inner):
    outer = rows // inner
    out, src = iota((rows, rows), 0), iota((rows, rows), 1)
    return one_hot(src == (out % outer) * inner + out // outer)


def natural_point(q):
    tile, lane = q // LANES, q % LANES
    return (4 * (lane // 16) + tile // 2) * BZ + 2 * (lane % 16) + tile % 2


def prepare_kernel(index_ref, local_ref, order_ref, pick_ref, local_out):
    order_ref[...] = one_hot(iota((PLANE, PLANE), 1) == natural_point(iota((PLANE, PLANE), 0)))
    index = index_ref[...]
    digits = jnp.concatenate([index // 32, index % 32] + [jnp.zeros((6, PLANE), jnp.int32)], axis=0)
    rows = jnp.concatenate([digits.astype(F32)] + [p.astype(F32) for p in split(local_ref[...], 3)], axis=0)
    moved = dot_nt(rows.astype(BF16), order_ref[...])
    local_out[...] = (moved[8:16] + moved[16:24]) + moved[24:32]
    index = (moved[0:1] * 32.0 + moved[1:2]).astype(jnp.int32)
    pick_ref[...] = one_hot(iota((PLANE, PLANE), 0) == index)


def prepare(line, plane_map, local):
    square = struct((PLANE, PLANE), BF16)
    return line.call(
        prepare_kernel, (square, square, struct((SLAB, PLANE), F32)), (plane_map, local), micros=2
    )


def relayout_kernel(core_hbm, out_ref, raw, mids, rows_ref, columns_ref, sems):
    def fetch(i):
        return pltpu.make_async_copy(core_hbm.at[pl.ds(i * 256, 256), :], raw.at[i], sems.at[i])

    for i in range(8):
        fetch(i).start()
    rows_ref[...] = row_permutation(256, SLAB)
    src, out = iota((256, 256), 0), iota((256, 256), 1)
    piece, low = out // PIECE, out % PIECE
    columns_ref[...] = one_hot(src == (4 * (low // 16) + piece // 2) * BZ + 2 * (low % 16) + piece % 2)
    lane = iota((PIECE, LANES), 1)
    half, quarter = lane < 64, lane % 64 < 32

    def permute(i, mid):
        for b in range(4):
            cols = pl.ds(b * 256, 256)
            ordered = dot(rows_ref[...], raw[i, :, cols]).astype(BF16)
            mid[:, cols] = dot(ordered, columns_ref[...]).astype(BF16)

    def gather(i, mid):
        at = pl.ds(pl.multiple_of(i * PIECE, PIECE), PIECE)
        for x in range(SLAB):
            for h in range(2):
                p = [
                    mid[pl.ds(x * PIECE, PIECE), pl.ds(b * 256 + h * LANES, LANES)]
                    for b in range(4)
                ]
                u = [jnp.where(half, p[k], pltpu.roll(p[k + 2], 64, 1)) for k in range(2)]
                v = [jnp.where(half, pltpu.roll(p[k], 64, 1), p[k + 2]) for k in range(2)]
                for k, (a, c) in enumerate((u, v)):
                    j = 4 * h + 2 * k
                    out_ref[x, at, pl.ds(j * LANES, LANES)] = jnp.where(
                        quarter, a, pltpu.roll(c, 32, 1)
                    )
                    out_ref[x, at, pl.ds((j + 1) * LANES, LANES)] = jnp.where(
                        quarter, pltpu.roll(a, LANES - 32, 1), c
                    )

    @pl.loop(0, CHUNKS // 4)
    def _(i):
        @pl.when(i < CHUNKS // 4 - 2)
        def _():
            for k in range(4):
                fetch(4 * i + 8 + k).start()

        for k in range(4):
            fetch(4 * i + k).wait()
        for k in range(5):
            if k < 4:
                permute(4 * i + k, mids.at[k])
            if k > 0:
                gather(4 * i + k - 1, mids.at[k - 1])


def relayout(line, core):
    square = pltpu.VMEM((256, 256), BF16)
    return line.call(
        relayout_kernel,
        (struct((SLAB, NCORE, PLANE), BF16),),
        (core.reshape(NCORE * SLAB, PLANE),),
        specs=[pl.BlockSpec(memory_space=pltpu.HBM)],
        scratch=[
            pltpu.VMEM((CHUNKS, 256, PLANE), BF16),
            pltpu.VMEM((4, 256, PLANE), BF16),
            square,
            square,
            pltpu.SemaphoreType.DMA((CHUNKS,)),
        ],
        limit=42,
        micros=8,
    )[0]


def sums(field_of, core_ref, full_ref, half_ref):
    for x in range(SLAB):
        part = dot_nt(field_of(x), core_ref[x])
        if x == 0:
            full_ref[...] = part
        else:
            full_ref[...] += part
    half_ref[...] = full_ref[...].astype(BF16)


def map_kernel(counts, pick_ref, core_ref, *refs):
    sources, (out_ref, full_ref, half_ref) = refs[:-3], refs[-3:]
    perm = row_permutation(BATCH * SLAB, SLAB)
    for b, count in enumerate(counts):
        value = sources[0][...]
        if count == 2:
            odd = lax.axis_index("group") % 2 == 1
            value = jnp.where(odd, value, sources[1][...])
        sources = sources[count:]
        got = dot(dot(perm, value).astype(BF16), pick_ref[...]).astype(BF16)
        out_ref[:, b * BATCH : (b + 1) * BATCH, :] = got.reshape(SLAB, BATCH, PLANE)
    sums(lambda x: out_ref[x], core_ref, full_ref, half_ref)


def map_batches(line, pick, core_x, batches):
    rows = BATCH * len(batches)
    counts = tuple(len(b) for b in batches)
    flat = [a.reshape(BATCH * SLAB, PLANE) for b in batches for a in b]
    return line.call(
        lambda *refs: map_kernel(counts, *refs),
        (struct((SLAB, rows, PLANE), BF16), struct((rows, NCORE), F32), struct((rows, NCORE), BF16)),
        (pick, core_x, *flat),
        micros=2 + len(batches) // 2,
    )


def exchange(half):
    return [
        lax.ppermute(half, "grid", [(i, i ^ k) for i in range(GRID)]) for k in range(1, GRID)
    ]


def total_of(full_ref, a_ref, b_ref, c_ref):
    rest = a_ref[...].astype(F32) + b_ref[...].astype(F32) + c_ref[...].astype(F32)
    return (full_ref[...] + rest).astype(BF16)


def project_kernel(full_ref, a_ref, b_ref, c_ref, field_ref, core_ref, *refs):
    local_ref = refs[0] if len(refs) == 4 else None
    out_ref, low_ref, high_ref = refs[-3:]
    coef = total_of(full_ref, a_ref, b_ref, c_ref)
    for x in range(SLAB):
        value = field_ref[x].astype(F32) - dot(coef, core_ref[x])
        out_ref[x] = value
        short = value.astype(BF16)
        if local_ref is not None:
            parts = [p.astype(F32) for p in split(local_ref[x : x + 1], 3)]
            rest = jnp.zeros((12, PLANE), F32)
            extra = jnp.concatenate(parts + [jnp.ones((1, PLANE), F32), rest], axis=0)
            short = jnp.concatenate([short, extra.astype(BF16)], axis=0)
        if x < HALO:
            low_ref[x] = short
        if x >= SLAB - HALO:
            high_ref[x - (SLAB - HALO)] = short


def project(line, full, others, field, core_x, local):
    rows = field.shape[1]
    sent = rows + (16 if local is not None else 0)
    return line.call(
        project_kernel,
        (
            struct((SLAB, rows, PLANE), F32),
            struct((HALO, sent, PLANE), BF16),
            struct((HALO, sent, PLANE), BF16),
        ),
        (full, *others, field, core_x) + ((local,) if local is not None else ()),
        micros=2,
    )


UP = [(i, i + 1) for i in range(GRID - 1)]
DOWN = [(j, i) for i, j in UP]


def filter_kernel(ahead, *refs):
    field_ref, below_ref, above_ref = refs[:3]
    if ahead:
        local_ref, weight_ref, first_ref, flag_ref, out_ref = refs[3:8]
    else:
        weight_ref, first_ref, flag_ref, core_ref, other_ref, out_ref, full_ref, half_ref = refs[3:11]
    below, above, even, odd = refs[-4:]
    rows = field_ref.shape[1]
    if ahead:
        weight_ref[HALO : HALO + SLAB] = 8.0 * local_ref[...] - 2.0
        for k, ref in enumerate((below_ref, above_ref)):
            for x in range(HALO):
                extra = ref[x, rows : rows + 16, :].astype(F32)
                near = (extra[0:1] + extra[1:2]) + extra[2:3]
                place = x if k == 0 else HALO + SLAB + x
                weight_ref[place : place + 1] = 8.0 * near - 2.0
                if x == 0:
                    flag_ref[k] = jnp.broadcast_to(extra[3:4, :LANES], (8, LANES))
        first_ref[...] = weight_ref[...] - EK[KDEG - 1]
    lane = iota((8, LANES), 1)
    head, tail = lane < 16, lane >= LANES - 16
    first_z, last_z = lane % 16 == 0, lane % 16 == 15
    low_flag, high_flag = flag_ref[0], flag_ref[1]

    def rolled(mask, value, by):
        return pltpu.roll(jnp.where(mask, 0.0, value), by % LANES, 1)

    def sweep(local, at):
        def begin(x, lanes):
            if x < HALO:
                return below[x, local, lanes]
            if x >= HALO + SLAB:
                return above[x - HALO - SLAB, local, lanes]
            return field_ref[x - HALO, at, lanes]

        def tiles(source, x):
            every = [pl.ds(j * LANES, LANES) for j in range(TILES)]
            if source is None:
                return [begin(x, lanes) for lanes in every]
            return [source[x, :, lanes] for lanes in every]

        source = None
        for k in range(1, KDEG + 1):
            target = even if k % 2 == 0 else odd
            first, last = k, WIDE - k
            here, after = tiles(source, first - 1), tiles(source, first)
            for x in range(first, last):
                before, here = here, after
                after = tiles(source, x + 1)
                up = [rolled(head, here[j], -16) for j in range(2)]
                down = [rolled(tail, here[j], 16) for j in range(6, 8)]
                for j in range(TILES):
                    lanes = pl.ds(j * LANES, LANES)
                    c = here[j]
                    above_y = here[j + 2] if j < 6 else up[j - 6]
                    below_y = here[j - 2] if j > 1 else down[j]
                    mate = here[j ^ 1]
                    z = mate + (rolled(first_z, mate, -1) if j % 2 else rolled(last_z, mate, 1))
                    around = (before[j] + after[j]) + (above_y + below_y) + z
                    w_ref = first_ref if k == 1 else weight_ref
                    w = jnp.broadcast_to(w_ref[pl.ds(x, 1), lanes], (8, LANES))
                    value = around - w * c
                    if k > 1:
                        value = value + EK[KDEG - k] * begin(x, lanes)
                    if x == HALO - 1:
                        value = value * low_flag
                    elif x == HALO + SLAB:
                        value = value * high_flag
                    if k == KDEG:
                        out_ref[x - HALO, at, lanes] = value * TOP
                    else:
                        target[x, :, lanes] = value
            source = target

    @pl.loop(0, rows // 16)
    def _(i):
        both = pl.ds(pl.multiple_of(i * 16, 16), 16)
        below[...] = below_ref[:, both, :].astype(F32)
        above[...] = above_ref[:, both, :].astype(F32)

        @pl.loop(0, 2)
        def _(k):
            sweep(
                pl.ds(pl.multiple_of(k * 8, 8), 8),
                pl.ds(pl.multiple_of(i * 16 + k * 8, 8), 8),
            )

    if not ahead:

        def both_of(x):
            return jnp.concatenate([other_ref[x].astype(BF16), out_ref[x].astype(BF16)], axis=0)

        sums(both_of, core_ref, full_ref, half_ref)


def filter_scratch():
    halo, whole = pltpu.VMEM((HALO, 16, PLANE), F32), pltpu.VMEM((WIDE, 8, PLANE), F32)
    return [halo, halo, whole, whole]


def filter_ahead(line, field, below, above, local):
    rows = field.shape[1]
    wide = struct((WIDE, PLANE), F32)
    got = line.call(
        lambda *refs: filter_kernel(True, *refs),
        (wide, wide, struct((2, 8, LANES), F32), struct((SLAB, rows, PLANE), F32)),
        (field, below, above, local),
        scratch=filter_scratch(),
        micros=7,
    )
    return got[:3], got[3]


def filter_rest(line, field, below, above, weight, core_x, ahead):
    rows = field.shape[1]
    total = rows + ahead.shape[1]
    return line.call(
        lambda *refs: filter_kernel(False, *refs),
        (struct((SLAB, rows, PLANE), F32), struct((total, NCORE), F32), struct((total, NCORE), BF16)),
        (field, below, above, *weight, core_x, ahead),
        scratch=filter_scratch(),
        micros=14,
    )


def reorder(value, order_ref):
    parts = split(value, 2)
    return dot(parts[0], order_ref[...]) + dot(parts[1], order_ref[...])


def clean_kernel(full_ref, a_ref, b_ref, c_ref, ahead_ref, rest_ref, mapped_ref, mapped_rest_ref, core_ref, order_ref, own_ref, density_ref, own, rows):
    coef = total_of(full_ref, a_ref, b_ref, c_ref)
    for x in range(SLAB):
        taken = dot(coef, core_ref[x])
        ahead = ahead_ref[x] - taken[:BATCH]
        rest = rest_ref[x] - taken[BATCH:]
        own[x * BATCH : (x + 1) * BATCH] = ahead
        weighted = jnp.sum(mapped_ref[x].astype(F32) * ahead, axis=0, keepdims=True)
        weighted += jnp.sum(mapped_rest_ref[x].astype(F32) * rest, axis=0, keepdims=True)
        rows[x : x + 1] = weighted / (3.0 * BATCH)
    back = row_permutation(BATCH * SLAB, BATCH)
    total = None
    for part in split(own[...], 2):
        moved = dot(dot(back, part).astype(BF16), order_ref[...])
        total = moved if total is None else total + moved
    own_ref[...] = total
    density_ref[...] = reorder(rows[...], order_ref)


def clean(line, full, others, ahead, rest, mapped, mapped_rest, core_x, order):
    small, own = struct((SLAB, PLANE), F32), struct((SLAB * BATCH, PLANE), F32)
    return line.call(
        clean_kernel,
        (own, small),
        (full, *others, ahead, rest, mapped, mapped_rest, core_x, order),
        scratch=[pltpu.VMEM(own.shape, F32), pltpu.VMEM(small.shape, F32)],
        limit=12,
        micros=4,
    )


def permute_groups(array, pairs):
    return lax.ppermute(array, "group", pairs)


def body(stochastic, plane_map, core_orbitals, potential):
    groups = lax.axis_size("group")
    mate = permute_groups(stochastic, [(i, i ^ 1) for i in range(groups)])
    third = permute_groups(stochastic, [(i, (i + 2) % groups) for i in range(groups)])

    line = Line()
    core_x = relayout(line, core_orbitals[0])
    order, pick, local = prepare(line, plane_map, potential[0])

    mate, line.token = lax.optimization_barrier((mate, line.token))
    second = permute_groups(mate, [(i, (i + 2) % groups) for i in range(0, groups, 2)])
    mapped, full, half = map_batches(line, pick, core_x, [(stochastic,)])
    others = exchange(half)
    field, low, high = project(line, full, others, mapped, core_x, local)
    below = lax.ppermute(high, "grid", UP)
    above = lax.ppermute(low, "grid", DOWN)

    batches = [(third,), (mate, second)]
    mapped_rest, full, half = map_batches(line, pick, core_x, batches)
    rest, low, high = project(line, full, exchange(half), mapped_rest, core_x, None)
    below_rest, above_rest = lax.ppermute(high, "grid", UP), lax.ppermute(low, "grid", DOWN)

    weight, ahead = filter_ahead(line, field, below, above, local)
    rest, full, half = filter_rest(line, rest, below_rest, above_rest, weight, core_x, ahead)
    own, density = clean(
        line, full, exchange(half), ahead, rest, mapped, mapped_rest, core_x, order
    )
    return density[None], own.reshape(BATCH, SLAB, PLANE)


def solution(mesh):
    return jax.shard_map(
        body,
        mesh=mesh,
        in_specs=(
            P("group", "grid", None),
            P("group", None),
            P("group", None, "grid", None),
            P("group", "grid", None),
        ),
        out_specs=(P("group", "grid", None), P("group", "grid", None)),
        check_vma=False,
    )
```

```python
from fractions import Fraction

import jax
import jax.numpy as jnp
from jax import lax
from jax.experimental import pallas as pl
from jax.experimental.pallas import tpu as pltpu
from jax.sharding import PartitionSpec as P


BZ = 32
KDEG = 6
BATCH = 32
NCORE = 512
SLAB = 8
PLANE = 1024
GRID = 4
HALO = KDEG
WIDE = SLAB + 2 * HALO
LANES = 128
TILES = PLANE // LANES
F32 = jnp.float32
BF16 = jnp.bfloat16


def horner_coefficients():
    cheb = [[Fraction(1)], [Fraction(0), Fraction(1)]]
    for _ in range(2, KDEG + 1):
        last, before = cheb[-1], cheb[-2]
        nxt = [Fraction(0)] + [2 * v for v in last]
        for i, v in enumerate(before):
            nxt[i] -= v
        cheb.append(nxt)
    mono = [Fraction(0)] * (KDEG + 1)
    for k, poly in enumerate(cheb):
        for i, v in enumerate(poly):
            mono[i] += v / (k + 1)
    scaled = [v / Fraction(-8) ** i for i, v in enumerate(mono)]
    top = scaled[KDEG]
    return [float(v / top) for v in scaled], float(top)


EK, TOP = horner_coefficients()

VMEM = pl.BlockSpec(memory_space=pltpu.VMEM)
ANY = pl.BlockSpec(memory_space=pl.ANY)
MIB = 1 << 20
PIECE = 32
SCALE = 500e6
CHUNKS = NCORE // PIECE
NT = (((1,), (1,)), ((), ()))


class Line:
    def __init__(self):
        self.token = None

    def call(self, kernel, out_shape, args, specs=None, scratch=(), limit=8, micros=2):
        specs = list(specs or [VMEM] * len(args))
        args = list(args)
        waits = self.token is not None
        if waits:
            args.append(self.token)
            specs.append(ANY)
        outs = tuple(out_shape) + (struct((8, LANES), F32),)

        def with_token(*refs):
            ins, rest = refs[: len(args)], refs[len(args) :]
            mine, token, extra = rest[: len(outs) - 1], rest[len(outs) - 1], rest[len(outs) :]
            kernel(*ins[: len(args) - waits], *mine, *extra)
            token[...] = jnp.zeros((8, LANES), F32)

        got = pl.pallas_call(
            with_token,
            in_specs=specs,
            out_specs=tuple(VMEM for _ in outs),
            out_shape=outs,
            scratch_shapes=list(scratch),
            compiler_params=pltpu.CompilerParams(vmem_limit_bytes=limit * MIB),
            cost_estimate=pl.CostEstimate(
                flops=int(micros * SCALE), bytes_accessed=1024, transcendentals=0
            ),
        )(*args)
        self.token = got[-1]
        return got[:-1]


def struct(shape, dtype):
    return jax.ShapeDtypeStruct(shape, dtype)


def one_hot(condition):
    return jnp.where(condition, 1.0, 0.0).astype(BF16)


def iota(shape, axis):
    return lax.broadcasted_iota(jnp.int32, shape, axis)


def dot(a, b):
    return jnp.dot(a, b, preferred_element_type=F32)


def dot_nt(a, b):
    return lax.dot_general(a, b, NT, preferred_element_type=F32)


def split(value, parts):
    out = []
    for _ in range(parts):
        out.append(value.astype(BF16))
        value = value - out[-1].astype(F32)
    return out


def row_permutation(rows, inner):
    outer = rows // inner
    out, src = iota((rows, rows), 0), iota((rows, rows), 1)
    return one_hot(src == (out % outer) * inner + out // outer)


def natural_point(q):
    tile, lane = q // LANES, q % LANES
    return (4 * (lane // 16) + tile // 2) * BZ + 2 * (lane % 16) + tile % 2


def prepare_kernel(index_ref, local_ref, order_ref, pick_ref, local_out):
    order_ref[...] = one_hot(iota((PLANE, PLANE), 1) == natural_point(iota((PLANE, PLANE), 0)))
    index = index_ref[...]
    digits = jnp.concatenate([index // 32, index % 32] + [jnp.zeros((6, PLANE), jnp.int32)], axis=0)
    rows = jnp.concatenate([digits.astype(F32)] + [p.astype(F32) for p in split(local_ref[...], 3)], axis=0)
    moved = dot_nt(rows.astype(BF16), order_ref[...])
    local_out[...] = (moved[8:16] + moved[16:24]) + moved[24:32]
    index = (moved[0:1] * 32.0 + moved[1:2]).astype(jnp.int32)
    pick_ref[...] = one_hot(iota((PLANE, PLANE), 0) == index)


def prepare(line, plane_map, local):
    square = struct((PLANE, PLANE), BF16)
    return line.call(
        prepare_kernel, (square, square, struct((SLAB, PLANE), F32)), (plane_map, local), micros=2
    )


def relayout_kernel(core_hbm, out_ref, raw, wide, columns_ref, sems):
    def fetch(i):
        return pltpu.make_async_copy(core_hbm.at[pl.ds(i * 256, 256), :], raw.at[i], sems.at[i])

    for i in range(8):
        fetch(i).start()
    src, out = iota((256, 256), 0), iota((256, 256), 1)
    for b in range(4):
        piece, low = 4 * (out // LANES) + (out // PIECE - b) % 4, out % PIECE
        columns_ref[b] = one_hot(
            src == (4 * (low // 16) + piece // 2) * BZ + 2 * (low % 16) + piece % 2
        )
    quarter = iota((PIECE, LANES), 1) // PIECE

    def permute(i, k):
        for b in range(4):
            moved = dot(raw[i, :, pl.ds(b * 256, 256)], columns_ref[b])
            wide[k, b, 0] = moved[:, :LANES]
            wide[k, b, 1] = moved[:, LANES:]

    def gather(i, k):
        at = pl.ds(pl.multiple_of(i * PIECE, PIECE), PIECE)
        for x in range(SLAB):
            rows = pl.ds(x, PIECE, stride=SLAB)
            for h in range(2):
                p = [wide[k, b, h, rows, :].astype(BF16) for b in range(4)]
                for q in range(4):
                    taken = p[3]
                    for b in range(3):
                        taken = jnp.where(quarter == (q + b) % 4, p[b], taken)
                    if q:
                        taken = pltpu.roll(taken, LANES - q * PIECE, 1)
                    out_ref[x, at, pl.ds((4 * h + q) * LANES, LANES)] = taken

    @pl.loop(0, CHUNKS // 4)
    def _(i):
        @pl.when(i < CHUNKS // 4 - 2)
        def _():
            for k in range(4):
                fetch(4 * i + 8 + k).start()

        for k in range(4):
            fetch(4 * i + k).wait()
        for k in range(5):
            if k < 4:
                permute(4 * i + k, k)
            if k > 0:
                gather(4 * i + k - 1, k - 1)


def relayout(line, core):
    return line.call(
        relayout_kernel,
        (struct((SLAB, NCORE, PLANE), BF16),),
        (core.reshape(NCORE * SLAB, PLANE),),
        specs=[pl.BlockSpec(memory_space=pltpu.HBM)],
        scratch=[
            pltpu.VMEM((CHUNKS, 256, PLANE), BF16),
            pltpu.VMEM((4, 4, 2, 256, LANES), F32),
            pltpu.VMEM((4, 256, 256), BF16),
            pltpu.SemaphoreType.DMA((CHUNKS,)),
        ],
        limit=42,
        micros=8,
    )[0]


def sums(field_of, core_ref, full_ref, half_ref):
    for x in range(SLAB):
        part = dot_nt(field_of(x), core_ref[x])
        if x == 0:
            full_ref[...] = part
        else:
            full_ref[...] += part
    half_ref[...] = full_ref[...].astype(BF16)


def map_kernel(counts, pick_ref, core_ref, *refs):
    sources, (out_ref, full_ref, half_ref) = refs[:-3], refs[-3:]
    perm = row_permutation(BATCH * SLAB, SLAB)
    for b, count in enumerate(counts):
        value = sources[0][...]
        if count == 2:
            odd = lax.axis_index("group") % 2 == 1
            value = jnp.where(odd, value, sources[1][...])
        sources = sources[count:]
        got = dot(dot(perm, value).astype(BF16), pick_ref[...]).astype(BF16)
        out_ref[:, b * BATCH : (b + 1) * BATCH, :] = got.reshape(SLAB, BATCH, PLANE)
    sums(lambda x: out_ref[x], core_ref, full_ref, half_ref)


def map_batches(line, pick, core_x, batches):
    rows = BATCH * len(batches)
    counts = tuple(len(b) for b in batches)
    flat = [a.reshape(BATCH * SLAB, PLANE) for b in batches for a in b]
    return line.call(
        lambda *refs: map_kernel(counts, *refs),
        (struct((SLAB, rows, PLANE), BF16), struct((rows, NCORE), F32), struct((rows, NCORE), BF16)),
        (pick, core_x, *flat),
        micros=2 + len(batches) // 2,
    )


def exchange(half):
    return [
        lax.ppermute(half, "grid", [(i, i ^ k) for i in range(GRID)]) for k in range(1, GRID)
    ]


def total_of(full_ref, a_ref, b_ref, c_ref):
    rest = a_ref[...].astype(F32) + b_ref[...].astype(F32) + c_ref[...].astype(F32)
    return (full_ref[...] + rest).astype(BF16)


def project_kernel(full_ref, a_ref, b_ref, c_ref, field_ref, core_ref, *refs):
    local_ref = refs[0] if len(refs) == 4 else None
    out_ref, low_ref, high_ref = refs[-3:]
    coef = total_of(full_ref, a_ref, b_ref, c_ref)
    for x in range(SLAB):
        value = field_ref[x].astype(F32) - dot(coef, core_ref[x])
        out_ref[x] = value
        short = value.astype(BF16)
        if local_ref is not None:
            parts = [p.astype(F32) for p in split(local_ref[x : x + 1], 3)]
            rest = jnp.zeros((12, PLANE), F32)
            extra = jnp.concatenate(parts + [jnp.ones((1, PLANE), F32), rest], axis=0)
            short = jnp.concatenate([short, extra.astype(BF16)], axis=0)
        if x < HALO:
            low_ref[x] = short
        if x >= SLAB - HALO:
            high_ref[x - (SLAB - HALO)] = short


def project(line, full, others, field, core_x, local):
    rows = field.shape[1]
    sent = rows + (16 if local is not None else 0)
    return line.call(
        project_kernel,
        (
            struct((SLAB, rows, PLANE), F32),
            struct((HALO, sent, PLANE), BF16),
            struct((HALO, sent, PLANE), BF16),
        ),
        (full, *others, field, core_x) + ((local,) if local is not None else ()),
        micros=2,
    )


UP = [(i, i + 1) for i in range(GRID - 1)]
DOWN = [(j, i) for i, j in UP]


def filter_kernel(ahead, *refs):
    field_ref, below_ref, above_ref = refs[:3]
    if ahead:
        local_ref, weight_ref, first_ref, flag_ref, out_ref = refs[3:8]
    else:
        weight_ref, first_ref, flag_ref, core_ref, other_ref, out_ref, full_ref, half_ref = refs[3:11]
    below, above, even, odd = refs[-4:]
    rows = field_ref.shape[1]
    if ahead:
        weight_ref[HALO : HALO + SLAB] = 8.0 * local_ref[...] - 2.0
        for k, ref in enumerate((below_ref, above_ref)):
            for x in range(HALO):
                extra = ref[x, rows : rows + 16, :].astype(F32)
                near = (extra[0:1] + extra[1:2]) + extra[2:3]
                place = x if k == 0 else HALO + SLAB + x
                weight_ref[place : place + 1] = 8.0 * near - 2.0
                if x == 0:
                    flag_ref[k] = jnp.broadcast_to(extra[3:4, :LANES], (8, LANES))
        first_ref[...] = weight_ref[...] - EK[KDEG - 1]
    lane = iota((8, LANES), 1)
    head, tail = lane < 16, lane >= LANES - 16
    first_z, last_z = lane % 16 == 0, lane % 16 == 15
    low_flag, high_flag = flag_ref[0], flag_ref[1]

    def rolled(mask, value, by):
        return pltpu.roll(jnp.where(mask, 0.0, value), by % LANES, 1)

    def sweep(local, at):
        def begin(x, lanes):
            if x < HALO:
                return below[x, local, lanes]
            if x >= HALO + SLAB:
                return above[x - HALO - SLAB, local, lanes]
            return field_ref[x - HALO, at, lanes]

        def tiles(source, x):
            every = [pl.ds(j * LANES, LANES) for j in range(TILES)]
            if source is None:
                return [begin(x, lanes) for lanes in every]
            return [source[x, :, lanes] for lanes in every]

        source = None
        for k in range(1, KDEG + 1):
            target = even if k % 2 == 0 else odd
            first, last = k, WIDE - k
            here, after = tiles(source, first - 1), tiles(source, first)
            for x in range(first, last):
                before, here = here, after
                after = tiles(source, x + 1)
                up = [rolled(head, here[j], -16) for j in range(2)]
                down = [rolled(tail, here[j], 16) for j in range(6, 8)]
                for j in range(TILES):
                    lanes = pl.ds(j * LANES, LANES)
                    c = here[j]
                    above_y = here[j + 2] if j < 6 else up[j - 6]
                    below_y = here[j - 2] if j > 1 else down[j]
                    mate = here[j ^ 1]
                    z = mate + (rolled(first_z, mate, -1) if j % 2 else rolled(last_z, mate, 1))
                    around = (before[j] + after[j]) + (above_y + below_y) + z
                    w_ref = first_ref if k == 1 else weight_ref
                    w = jnp.broadcast_to(w_ref[pl.ds(x, 1), lanes], (8, LANES))
                    value = around - w * c
                    if k > 1:
                        value = value + EK[KDEG - k] * begin(x, lanes)
                    if x == HALO - 1:
                        value = value * low_flag
                    elif x == HALO + SLAB:
                        value = value * high_flag
                    if k == KDEG:
                        out_ref[x - HALO, at, lanes] = value * TOP
                    else:
                        target[x, :, lanes] = value
            source = target

    @pl.loop(0, rows // 16)
    def _(i):
        both = pl.ds(pl.multiple_of(i * 16, 16), 16)
        below[...] = below_ref[:, both, :].astype(F32)
        above[...] = above_ref[:, both, :].astype(F32)

        @pl.loop(0, 2)
        def _(k):
            sweep(
                pl.ds(pl.multiple_of(k * 8, 8), 8),
                pl.ds(pl.multiple_of(i * 16 + k * 8, 8), 8),
            )

    if not ahead:

        def both_of(x):
            return jnp.concatenate([other_ref[x].astype(BF16), out_ref[x].astype(BF16)], axis=0)

        sums(both_of, core_ref, full_ref, half_ref)


def filter_scratch():
    halo, whole = pltpu.VMEM((HALO, 16, PLANE), F32), pltpu.VMEM((WIDE, 8, PLANE), F32)
    return [halo, halo, whole, whole]


def filter_ahead(line, field, below, above, local):
    rows = field.shape[1]
    wide = struct((WIDE, PLANE), F32)
    got = line.call(
        lambda *refs: filter_kernel(True, *refs),
        (wide, wide, struct((2, 8, LANES), F32), struct((SLAB, rows, PLANE), F32)),
        (field, below, above, local),
        scratch=filter_scratch(),
        micros=7,
    )
    return got[:3], got[3]


def filter_rest(line, field, below, above, weight, core_x, ahead):
    rows = field.shape[1]
    total = rows + ahead.shape[1]
    return line.call(
        lambda *refs: filter_kernel(False, *refs),
        (struct((SLAB, rows, PLANE), F32), struct((total, NCORE), F32), struct((total, NCORE), BF16)),
        (field, below, above, *weight, core_x, ahead),
        scratch=filter_scratch(),
        micros=14,
    )


def reorder(value, order_ref):
    parts = split(value, 2)
    return dot(parts[0], order_ref[...]) + dot(parts[1], order_ref[...])


def clean_kernel(full_ref, a_ref, b_ref, c_ref, ahead_ref, rest_ref, mapped_ref, mapped_rest_ref, core_ref, order_ref, own_ref, density_ref, own, rows):
    coef = total_of(full_ref, a_ref, b_ref, c_ref)
    for x in range(SLAB):
        taken = dot(coef, core_ref[x])
        ahead = ahead_ref[x] - taken[: ahead_ref.shape[1]]
        rest = rest_ref[x] - taken[ahead_ref.shape[1] :]
        own[x * BATCH : (x + 1) * BATCH] = ahead[:BATCH]
        weighted = jnp.sum(mapped_ref[x].astype(F32) * ahead, axis=0, keepdims=True)
        weighted += jnp.sum(mapped_rest_ref[x].astype(F32) * rest, axis=0, keepdims=True)
        rows[x : x + 1] = weighted / (3.0 * BATCH)
    back = row_permutation(BATCH * SLAB, BATCH)
    total = None
    for part in split(own[...], 2):
        moved = dot(dot(back, part).astype(BF16), order_ref[...])
        total = moved if total is None else total + moved
    own_ref[...] = total
    density_ref[...] = reorder(rows[...], order_ref)


def clean(line, full, others, ahead, rest, mapped, mapped_rest, core_x, order):
    small, own = struct((SLAB, PLANE), F32), struct((SLAB * BATCH, PLANE), F32)
    return line.call(
        clean_kernel,
        (own, small),
        (full, *others, ahead, rest, mapped, mapped_rest, core_x, order),
        scratch=[pltpu.VMEM(own.shape, F32), pltpu.VMEM(small.shape, F32)],
        limit=12,
        micros=4,
    )


def permute_groups(array, pairs):
    return lax.ppermute(array, "group", pairs)


def body(stochastic, plane_map, core_orbitals, potential):
    groups = lax.axis_size("group")
    mate = permute_groups(stochastic, [(i, i ^ 1) for i in range(groups)])
    third = permute_groups(stochastic, [(i, (i + 2) % groups) for i in range(groups)])

    line = Line()
    core_x = relayout(line, core_orbitals[0])
    order, pick, local = prepare(line, plane_map, potential[0])

    mate, line.token = lax.optimization_barrier((mate, line.token))
    second = permute_groups(mate, [(i, (i + 2) % groups) for i in range(0, groups, 2)])
    mapped, full, half = map_batches(line, pick, core_x, [(stochastic,), (third,)])
    others = exchange(half)
    field, low, high = project(line, full, others, mapped, core_x, local)
    below = lax.ppermute(high, "grid", UP)
    above = lax.ppermute(low, "grid", DOWN)

    mapped_rest, full, half = map_batches(line, pick, core_x, [(mate, second)])
    others = exchange(half)
    rest, low, high = project(line, full, others, mapped_rest, core_x, None)
    below_rest, above_rest = lax.ppermute(high, "grid", UP), lax.ppermute(low, "grid", DOWN)

    weight, ahead = filter_ahead(line, field, below, above, local)
    rest, full, half = filter_rest(line, rest, below_rest, above_rest, weight, core_x, ahead)
    own, density = clean(
        line, full, exchange(half), ahead, rest, mapped, mapped_rest, core_x, order
    )
    return density[None], own.reshape(BATCH, SLAB, PLANE)


def solution(mesh):
    return jax.shard_map(
        body,
        mesh=mesh,
        in_specs=(
            P("group", "grid", None),
            P("group", None),
            P("group", None, "grid", None),
            P("group", "grid", None),
        ),
        out_specs=(P("group", "grid", None), P("group", "grid", None)),
        check_vma=False,
    )
```

```python
from fractions import Fraction

import jax
import jax.numpy as jnp
from jax import lax
from jax.experimental import pallas as pl
from jax.experimental.pallas import tpu as pltpu
from jax.sharding import PartitionSpec as P


BZ = 32
KDEG = 6
BATCH = 32
NCORE = 512
SLAB = 8
PLANE = 1024
GRID = 4
HALO = KDEG
WIDE = SLAB + 2 * HALO
LANES = 128
TILES = PLANE // LANES
F32 = jnp.float32
BF16 = jnp.bfloat16


def horner_coefficients():
    cheb = [[Fraction(1)], [Fraction(0), Fraction(1)]]
    for _ in range(2, KDEG + 1):
        last, before = cheb[-1], cheb[-2]
        nxt = [Fraction(0)] + [2 * v for v in last]
        for i, v in enumerate(before):
            nxt[i] -= v
        cheb.append(nxt)
    mono = [Fraction(0)] * (KDEG + 1)
    for k, poly in enumerate(cheb):
        for i, v in enumerate(poly):
            mono[i] += v / (k + 1)
    scaled = [v / Fraction(-8) ** i for i, v in enumerate(mono)]
    top = scaled[KDEG]
    return [float(v / top) for v in scaled], float(top)


EK, TOP = horner_coefficients()

VMEM = pl.BlockSpec(memory_space=pltpu.VMEM)
ANY = pl.BlockSpec(memory_space=pl.ANY)
MIB = 1 << 20
PIECE = 32
SCALE = 500e6
EXTRA = 8
CHUNKS = NCORE // PIECE
NT = (((1,), (1,)), ((), ()))


class Line:
    def __init__(self):
        self.token = None

    def call(self, kernel, out_shape, args, specs=None, scratch=(), limit=8, micros=2):
        specs = list(specs or [VMEM] * len(args))
        args = list(args)
        waits = self.token is not None
        if waits:
            args.append(self.token)
            specs.append(ANY)
        outs = tuple(out_shape) + (struct((8, LANES), F32),)

        def with_token(*refs):
            ins, rest = refs[: len(args)], refs[len(args) :]
            mine, token, extra = rest[: len(outs) - 1], rest[len(outs) - 1], rest[len(outs) :]
            kernel(*ins[: len(args) - waits], *mine, *extra)
            token[...] = jnp.zeros((8, LANES), F32)

        got = pl.pallas_call(
            with_token,
            in_specs=specs,
            out_specs=tuple(VMEM for _ in outs),
            out_shape=outs,
            scratch_shapes=list(scratch),
            compiler_params=pltpu.CompilerParams(vmem_limit_bytes=limit * MIB),
            cost_estimate=pl.CostEstimate(
                flops=int(micros * SCALE), bytes_accessed=1024, transcendentals=0
            ),
        )(*args)
        self.token = got[-1]
        return got[:-1]


def struct(shape, dtype):
    return jax.ShapeDtypeStruct(shape, dtype)


def one_hot(condition):
    return jnp.where(condition, 1.0, 0.0).astype(BF16)


def iota(shape, axis):
    return lax.broadcasted_iota(jnp.int32, shape, axis)


def dot(a, b):
    return jnp.dot(a, b, preferred_element_type=F32)


def dot_nt(a, b):
    return lax.dot_general(a, b, NT, preferred_element_type=F32)


def split(value, parts):
    out = []
    for _ in range(parts):
        out.append(value.astype(BF16))
        value = value - out[-1].astype(F32)
    return out


def row_permutation(rows, inner):
    outer = rows // inner
    out, src = iota((rows, rows), 0), iota((rows, rows), 1)
    return one_hot(src == (out % outer) * inner + out // outer)


def natural_point(q):
    tile, lane = q // LANES, q % LANES
    return (4 * (lane // 16) + tile // 2) * BZ + 2 * (lane % 16) + tile % 2


def prepare_kernel(index_ref, local_ref, order_ref, pick_ref, local_out):
    order_ref[...] = one_hot(iota((PLANE, PLANE), 1) == natural_point(iota((PLANE, PLANE), 0)))
    index = index_ref[...]
    digits = jnp.concatenate([index // 32, index % 32] + [jnp.zeros((6, PLANE), jnp.int32)], axis=0)
    rows = jnp.concatenate([digits.astype(F32)] + [p.astype(F32) for p in split(local_ref[...], 3)], axis=0)
    moved = dot_nt(rows.astype(BF16), order_ref[...])
    local_out[...] = (moved[8:16] + moved[16:24]) + moved[24:32]
    index = (moved[0:1] * 32.0 + moved[1:2]).astype(jnp.int32)
    pick_ref[...] = one_hot(iota((PLANE, PLANE), 0) == index)


def prepare(line, plane_map, local):
    square = struct((PLANE, PLANE), BF16)
    return line.call(
        prepare_kernel, (square, square, struct((SLAB, PLANE), F32)), (plane_map, local), micros=2
    )


def relayout_kernel(core_hbm, out_ref, raw, wide, columns_ref, sems):
    def fetch(i):
        return pltpu.make_async_copy(core_hbm.at[pl.ds(i * 256, 256), :], raw.at[i], sems.at[i])

    for i in range(8):
        fetch(i).start()
    src, out = iota((256, 256), 0), iota((256, 256), 1)
    for b in range(4):
        piece, low = 4 * (out // LANES) + (out // PIECE - b) % 4, out % PIECE
        columns_ref[b] = one_hot(
            src == (4 * (low // 16) + piece // 2) * BZ + 2 * (low % 16) + piece % 2
        )
    quarter = iota((PIECE, LANES), 1) // PIECE

    def permute(i, k):
        for b in range(4):
            moved = dot(raw[i, :, pl.ds(b * 256, 256)], columns_ref[b])
            wide[k, b, 0] = moved[:, :LANES]
            wide[k, b, 1] = moved[:, LANES:]

    def gather(i, k):
        at = pl.ds(pl.multiple_of(i * PIECE, PIECE), PIECE)
        for x in range(SLAB):
            rows = pl.ds(x, PIECE, stride=SLAB)
            for h in range(2):
                p = [wide[k, b, h, rows, :].astype(BF16) for b in range(4)]
                for q in range(4):
                    taken = p[3]
                    for b in range(3):
                        taken = jnp.where(quarter == (q + b) % 4, p[b], taken)
                    if q:
                        taken = pltpu.roll(taken, LANES - q * PIECE, 1)
                    out_ref[x, at, pl.ds((4 * h + q) * LANES, LANES)] = taken

    @pl.loop(0, CHUNKS // 4)
    def _(i):
        @pl.when(i < CHUNKS // 4 - 2)
        def _():
            for k in range(4):
                fetch(4 * i + 8 + k).start()

        for k in range(4):
            fetch(4 * i + k).wait()
        for k in range(5):
            if k < 4:
                permute(4 * i + k, k)
            if k > 0:
                gather(4 * i + k - 1, k - 1)


def relayout(line, core):
    return line.call(
        relayout_kernel,
        (struct((SLAB, NCORE, PLANE), BF16),),
        (core.reshape(NCORE * SLAB, PLANE),),
        specs=[pl.BlockSpec(memory_space=pltpu.HBM)],
        scratch=[
            pltpu.VMEM((CHUNKS, 256, PLANE), BF16),
            pltpu.VMEM((4, 4, 2, 256, LANES), F32),
            pltpu.VMEM((4, 256, 256), BF16),
            pltpu.SemaphoreType.DMA((CHUNKS,)),
        ],
        limit=42,
        micros=8,
    )[0]


def sums(field_of, core_ref, full_ref, half_ref):
    for x in range(SLAB):
        part = dot_nt(field_of(x), core_ref[x])
        if x == 0:
            full_ref[...] = part
        else:
            full_ref[...] += part
    half_ref[...] = full_ref[...].astype(BF16)


def map_kernel(counts, pick_ref, core_ref, *refs):
    sources, (out_ref, full_ref, half_ref) = refs[:-3], refs[-3:]
    perm = row_permutation(BATCH * SLAB, SLAB)
    for b, count in enumerate(counts):
        value = sources[0][...]
        if count == 2:
            odd = lax.axis_index("group") % 2 == 1
            value = jnp.where(odd, value, sources[1][...])
        sources = sources[count:]
        got = dot(dot(perm, value).astype(BF16), pick_ref[...]).astype(BF16)
        out_ref[:, b * BATCH : (b + 1) * BATCH, :] = got.reshape(SLAB, BATCH, PLANE)
    sums(lambda x: out_ref[x], core_ref, full_ref, half_ref)


def map_batches(line, pick, core_x, batches):
    rows = BATCH * len(batches)
    counts = tuple(len(b) for b in batches)
    flat = [a.reshape(BATCH * SLAB, PLANE) for b in batches for a in b]
    return line.call(
        lambda *refs: map_kernel(counts, *refs),
        (struct((SLAB, rows, PLANE), BF16), struct((rows, NCORE), F32), struct((rows, NCORE), BF16)),
        (pick, core_x, *flat),
        micros=2 + len(batches) // 2,
    )


def exchange(half):
    return [
        lax.ppermute(half, "grid", [(i, i ^ k) for i in range(GRID)]) for k in range(1, GRID)
    ]


def total_of(full_ref, a_ref, b_ref, c_ref):
    rest = a_ref[...].astype(F32) + b_ref[...].astype(F32) + c_ref[...].astype(F32)
    return (full_ref[...] + rest).astype(BF16)


def project_kernel(full_ref, a_ref, b_ref, c_ref, field_ref, core_ref, *refs):
    local_ref = refs[0] if len(refs) == 4 else None
    out_ref, low_ref, high_ref = refs[-3:]
    coef = total_of(full_ref, a_ref, b_ref, c_ref)
    for x in range(SLAB):
        value = field_ref[x].astype(F32) - dot(coef, core_ref[x])
        out_ref[x] = value
        short = value.astype(BF16)
        if local_ref is not None:
            parts = [p.astype(F32) for p in split(local_ref[x : x + 1], 3)]
            rest = jnp.zeros((EXTRA - 4, PLANE), F32)
            extra = jnp.concatenate(parts + [jnp.ones((1, PLANE), F32), rest], axis=0)
            short = jnp.concatenate([short, extra.astype(BF16)], axis=0)
        if x < HALO:
            low_ref[x] = short
        if x >= SLAB - HALO:
            high_ref[x - (SLAB - HALO)] = short


def project(line, full, others, field, core_x, local):
    rows = field.shape[1]
    sent = rows + (EXTRA if local is not None else 0)
    return line.call(
        project_kernel,
        (
            struct((SLAB, rows, PLANE), F32),
            struct((HALO, sent, PLANE), BF16),
            struct((HALO, sent, PLANE), BF16),
        ),
        (full, *others, field, core_x) + ((local,) if local is not None else ()),
        micros=2,
    )


UP = [(i, i + 1) for i in range(GRID - 1)]
DOWN = [(j, i) for i, j in UP]


def filter_kernel(mode, offset, *refs):
    field_ref, below_ref, above_ref = refs[:3]
    others = ()
    if mode == "first":
        local_ref, weight_ref, first_ref, flag_ref, out_ref = refs[3:8]
    elif mode == "more":
        weight_ref, first_ref, flag_ref, out_ref = refs[3:7]
    else:
        weight_ref, first_ref, flag_ref, core_ref = refs[3:7]
        others, (out_ref, full_ref, half_ref) = refs[7:-7], refs[-7:-4]
    below, above, even, odd = refs[-4:]
    rows = field_ref.shape[1]
    if mode == "first":
        weight_ref[HALO : HALO + SLAB] = 8.0 * local_ref[...] - 2.0
        for k, ref in enumerate((below_ref, above_ref)):
            for x in range(HALO):
                extra = ref[x, rows : rows + EXTRA, :].astype(F32)
                near = (extra[0:1] + extra[1:2]) + extra[2:3]
                place = x if k == 0 else HALO + SLAB + x
                weight_ref[place : place + 1] = 8.0 * near - 2.0
                if x == 0:
                    flag_ref[k] = jnp.broadcast_to(extra[3:4, :LANES], (8, LANES))
        first_ref[...] = weight_ref[...] - EK[KDEG - 1]
    lane = iota((8, LANES), 1)
    head, tail = lane < 16, lane >= LANES - 16
    first_z, last_z = lane % 16 == 0, lane % 16 == 15
    low_flag, high_flag = flag_ref[0], flag_ref[1]

    def rolled(mask, value, by):
        return pltpu.roll(jnp.where(mask, 0.0, value), by % LANES, 1)

    def sweep(local, at, put):
        def begin(x, lanes):
            if x < HALO:
                return below[x, local, lanes]
            if x >= HALO + SLAB:
                return above[x - HALO - SLAB, local, lanes]
            return field_ref[x - HALO, at, lanes]

        def tiles(source, x):
            every = [pl.ds(j * LANES, LANES) for j in range(TILES)]
            if source is None:
                return [begin(x, lanes) for lanes in every]
            return [source[x, :, lanes] for lanes in every]

        source = None
        for k in range(1, KDEG + 1):
            target = even if k % 2 == 0 else odd
            first, last = k, WIDE - k
            here, after = tiles(source, first - 1), tiles(source, first)
            for x in range(first, last):
                before, here = here, after
                after = tiles(source, x + 1)
                up = [rolled(head, here[j], -16) for j in range(2)]
                down = [rolled(tail, here[j], 16) for j in range(6, 8)]
                for j in range(TILES):
                    lanes = pl.ds(j * LANES, LANES)
                    c = here[j]
                    above_y = here[j + 2] if j < 6 else up[j - 6]
                    below_y = here[j - 2] if j > 1 else down[j]
                    mate = here[j ^ 1]
                    z = mate + (rolled(first_z, mate, -1) if j % 2 else rolled(last_z, mate, 1))
                    around = (before[j] + after[j]) + (above_y + below_y) + z
                    w_ref = first_ref if k == 1 else weight_ref
                    w = jnp.broadcast_to(w_ref[pl.ds(x, 1), lanes], (8, LANES))
                    value = around - w * c
                    if k > 1:
                        value = value + EK[KDEG - k] * begin(x, lanes)
                    if x == HALO - 1:
                        value = value * low_flag
                    elif x == HALO + SLAB:
                        value = value * high_flag
                    if k == KDEG:
                        out_ref[x - HALO, put, lanes] = value * TOP
                    else:
                        target[x, :, lanes] = value
            source = target

    @pl.loop(0, out_ref.shape[1] // 16)
    def _(i):
        both = pl.ds(pl.multiple_of(offset + i * 16, 16), 16)
        below[...] = below_ref[:, both, :].astype(F32)
        above[...] = above_ref[:, both, :].astype(F32)

        @pl.loop(0, 2)
        def _(k):
            sweep(
                pl.ds(pl.multiple_of(k * 8, 8), 8),
                pl.ds(pl.multiple_of(offset + i * 16 + k * 8, 8), 8),
                pl.ds(pl.multiple_of(i * 16 + k * 8, 8), 8),
            )

    if mode == "last":

        def all_of(x):
            return jnp.concatenate([r[x].astype(BF16) for r in (*others, out_ref)], axis=0)

        sums(all_of, core_ref, full_ref, half_ref)


def filter_scratch():
    halo, whole = pltpu.VMEM((HALO, 16, PLANE), F32), pltpu.VMEM((WIDE, 8, PLANE), F32)
    return [halo, halo, whole, whole]


def filter_first(line, field, below, above, local):
    wide = struct((WIDE, PLANE), F32)
    got = line.call(
        lambda *refs: filter_kernel("first", 0, *refs),
        (wide, wide, struct((2, 8, LANES), F32), struct((SLAB, BATCH, PLANE), F32)),
        (field, below, above, local),
        scratch=filter_scratch(),
        micros=6,
    )
    return got[:3], got[3]


def filter_more(line, field, below, above, weight):
    return line.call(
        lambda *refs: filter_kernel("more", BATCH, *refs),
        (struct((SLAB, BATCH, PLANE), F32),),
        (field, below, above, *weight),
        scratch=filter_scratch(),
        micros=6,
    )[0]


def filter_last(line, field, below, above, weight, core_x, others):
    total = BATCH * (1 + len(others))
    return line.call(
        lambda *refs: filter_kernel("last", 0, *refs),
        (struct((SLAB, BATCH, PLANE), F32), struct((total, NCORE), F32), struct((total, NCORE), BF16)),
        (field, below, above, *weight, core_x, *others),
        scratch=filter_scratch(),
        micros=8,
    )


def reorder(value, order_ref):
    parts = split(value, 2)
    return dot(parts[0], order_ref[...]) + dot(parts[1], order_ref[...])


def clean_kernel(full_ref, a_ref, b_ref, c_ref, first_ref, more_ref, last_ref, mapped_ref, mapped_rest_ref, core_ref, order_ref, own_ref, density_ref, own, rows):
    coef = total_of(full_ref, a_ref, b_ref, c_ref)
    for x in range(SLAB):
        taken = dot(coef, core_ref[x])
        mapped = (mapped_ref[x, :BATCH], mapped_ref[x, BATCH:], mapped_rest_ref[x])
        total = None
        for t, ref in enumerate((first_ref, more_ref, last_ref)):
            value = ref[x] - taken[t * BATCH : (t + 1) * BATCH]
            if t == 0:
                own[x * BATCH : (x + 1) * BATCH] = value
            term = mapped[t].astype(F32) * value
            total = term if total is None else total + term
        rows[x : x + 1] = jnp.sum(total, axis=0, keepdims=True) / (3.0 * BATCH)
    back = row_permutation(BATCH * SLAB, BATCH)
    total = None
    for part in split(own[...], 2):
        moved = dot(dot(back, part).astype(BF16), order_ref[...])
        total = moved if total is None else total + moved
    own_ref[...] = total
    density_ref[...] = reorder(rows[...], order_ref)


def clean(line, full, others, fields, mapped, mapped_rest, core_x, order):
    small, own = struct((SLAB, PLANE), F32), struct((SLAB * BATCH, PLANE), F32)
    return line.call(
        clean_kernel,
        (own, small),
        (full, *others, *fields, mapped, mapped_rest, core_x, order),
        scratch=[pltpu.VMEM(own.shape, F32), pltpu.VMEM(small.shape, F32)],
        limit=12,
        micros=4,
    )


def permute_groups(array, pairs):
    return lax.ppermute(array, "group", pairs)


def body(stochastic, plane_map, core_orbitals, potential):
    groups = lax.axis_size("group")
    mate = permute_groups(stochastic, [(i, i ^ 1) for i in range(groups)])
    third = permute_groups(stochastic, [(i, (i + 2) % groups) for i in range(groups)])

    line = Line()
    core_x = relayout(line, core_orbitals[0])
    order, pick, local = prepare(line, plane_map, potential[0])

    mate, line.token = lax.optimization_barrier((mate, line.token))
    second = permute_groups(mate, [(i, (i + 2) % groups) for i in range(0, groups, 2)])
    mapped, full, half = map_batches(line, pick, core_x, [(stochastic,), (third,)])
    others = exchange(half)
    field, low, high = project(line, full, others, mapped, core_x, local)
    below = lax.ppermute(high, "grid", UP)
    above = lax.ppermute(low, "grid", DOWN)

    mapped_rest, full, half = map_batches(line, pick, core_x, [(mate, second)])
    others = exchange(half)
    weight, first = filter_first(line, field, below, above, local)
    rest, low, high = project(line, full, others, mapped_rest, core_x, None)
    below_rest = lax.ppermute(high, "grid", UP)
    above_rest = lax.ppermute(low, "grid", DOWN)
    more = filter_more(line, field, below, above, weight)
    last, full, half = filter_last(
        line, rest, below_rest, above_rest, weight, core_x, (first, more)
    )
    fields = (first, more, last)
    own, density = clean(line, full, exchange(half), fields, mapped, mapped_rest, core_x, order)
    return density[None], own.reshape(BATCH, SLAB, PLANE)


def solution(mesh):
    return jax.shard_map(
        body,
        mesh=mesh,
        in_specs=(
            P("group", "grid", None),
            P("group", None),
            P("group", None, "grid", None),
            P("group", "grid", None),
        ),
        out_specs=(P("group", "grid", None), P("group", "grid", None)),
        check_vma=False,
    )
```

```python
from fractions import Fraction

import jax
import jax.numpy as jnp
from jax import lax
from jax.experimental import pallas as pl
from jax.experimental.pallas import tpu as pltpu
from jax.sharding import PartitionSpec as P


BZ = 32
KDEG = 6
BATCH = 32
NCORE = 512
SLAB = 8
PLANE = 1024
GRID = 4
HALO = KDEG
WIDE = SLAB + 2 * HALO
LANES = 128
TILES = PLANE // LANES
F32 = jnp.float32
BF16 = jnp.bfloat16


def horner_coefficients():
    cheb = [[Fraction(1)], [Fraction(0), Fraction(1)]]
    for _ in range(2, KDEG + 1):
        last, before = cheb[-1], cheb[-2]
        nxt = [Fraction(0)] + [2 * v for v in last]
        for i, v in enumerate(before):
            nxt[i] -= v
        cheb.append(nxt)
    mono = [Fraction(0)] * (KDEG + 1)
    for k, poly in enumerate(cheb):
        for i, v in enumerate(poly):
            mono[i] += v / (k + 1)
    scaled = [v / Fraction(-8) ** i for i, v in enumerate(mono)]
    top = scaled[KDEG]
    return [float(v / top) for v in scaled], float(top)


EK, TOP = horner_coefficients()

VMEM = pl.BlockSpec(memory_space=pltpu.VMEM)
ANY = pl.BlockSpec(memory_space=pl.ANY)
MIB = 1 << 20
PIECE = 32
SCALE = 500e6
EXTRA = 8
CHUNKS = NCORE // PIECE
NT = (((1,), (1,)), ((), ()))


class Line:
    def __init__(self):
        self.token = None

    def call(self, kernel, out_shape, args, specs=None, scratch=(), limit=8, micros=2):
        specs = list(specs or [VMEM] * len(args))
        args = list(args)
        waits = self.token is not None
        if waits:
            args.append(self.token)
            specs.append(ANY)
        outs = tuple(out_shape) + (struct((8, LANES), F32),)

        def with_token(*refs):
            ins, rest = refs[: len(args)], refs[len(args) :]
            mine, token, extra = rest[: len(outs) - 1], rest[len(outs) - 1], rest[len(outs) :]
            kernel(*ins[: len(args) - waits], *mine, *extra)
            token[...] = jnp.zeros((8, LANES), F32)

        got = pl.pallas_call(
            with_token,
            in_specs=specs,
            out_specs=tuple(VMEM for _ in outs),
            out_shape=outs,
            scratch_shapes=list(scratch),
            compiler_params=pltpu.CompilerParams(vmem_limit_bytes=limit * MIB),
            cost_estimate=pl.CostEstimate(
                flops=int(micros * SCALE), bytes_accessed=1024, transcendentals=0
            ),
        )(*args)
        self.token = got[-1]
        return got[:-1]


def struct(shape, dtype):
    return jax.ShapeDtypeStruct(shape, dtype)


def one_hot(condition):
    return jnp.where(condition, 1.0, 0.0).astype(BF16)


def iota(shape, axis):
    return lax.broadcasted_iota(jnp.int32, shape, axis)


def dot(a, b):
    return jnp.dot(a, b, preferred_element_type=F32)


def dot_nt(a, b):
    return lax.dot_general(a, b, NT, preferred_element_type=F32)


def split(value, parts):
    out = []
    for _ in range(parts):
        out.append(value.astype(BF16))
        value = value - out[-1].astype(F32)
    return out


def row_permutation(rows, inner):
    outer = rows // inner
    out, src = iota((rows, rows), 0), iota((rows, rows), 1)
    return one_hot(src == (out % outer) * inner + out // outer)


def natural_point(q):
    tile, lane = q // LANES, q % LANES
    return (4 * (lane // 16) + tile // 2) * BZ + 2 * (lane % 16) + tile % 2


def prepare_kernel(index_ref, local_ref, order_ref, pick_ref, local_out):
    order_ref[...] = one_hot(iota((PLANE, PLANE), 1) == natural_point(iota((PLANE, PLANE), 0)))
    index = index_ref[...]
    digits = jnp.concatenate([index // 32, index % 32] + [jnp.zeros((6, PLANE), jnp.int32)], axis=0)
    rows = jnp.concatenate([digits.astype(F32)] + [p.astype(F32) for p in split(local_ref[...], 3)], axis=0)
    moved = dot_nt(rows.astype(BF16), order_ref[...])
    local_out[...] = (moved[8:16] + moved[16:24]) + moved[24:32]
    index = (moved[0:1] * 32.0 + moved[1:2]).astype(jnp.int32)
    pick_ref[...] = one_hot(iota((PLANE, PLANE), 0) == index)


def prepare(line, plane_map, local):
    square = struct((PLANE, PLANE), BF16)
    return line.call(
        prepare_kernel, (square, square, struct((SLAB, PLANE), F32)), (plane_map, local), micros=2
    )


def relayout_kernel(core_hbm, out_ref, raw, wide, columns_ref, sems):
    def fetch(i):
        return pltpu.make_async_copy(core_hbm.at[pl.ds(i * 256, 256), :], raw.at[i], sems.at[i])

    for i in range(8):
        fetch(i).start()
    src, out = iota((256, 256), 0), iota((256, 256), 1)
    for b in range(4):
        piece, low = 4 * (out // LANES) + (out // PIECE - b) % 4, out % PIECE
        columns_ref[b] = one_hot(
            src == (4 * (low // 16) + piece // 2) * BZ + 2 * (low % 16) + piece % 2
        )
    quarter = iota((PIECE, LANES), 1) // PIECE

    def permute(i, k):
        for b in range(4):
            moved = dot(raw[i, :, pl.ds(b * 256, 256)], columns_ref[b])
            wide[k, b, 0] = moved[:, :LANES]
            wide[k, b, 1] = moved[:, LANES:]

    def gather(i, k):
        at = pl.ds(pl.multiple_of(i * PIECE, PIECE), PIECE)
        for x in range(SLAB):
            rows = pl.ds(x, PIECE, stride=SLAB)
            for h in range(2):
                p = [wide[k, b, h, rows, :].astype(BF16) for b in range(4)]
                for q in range(4):
                    taken = p[3]
                    for b in range(3):
                        taken = jnp.where(quarter == (q + b) % 4, p[b], taken)
                    if q:
                        taken = pltpu.roll(taken, LANES - q * PIECE, 1)
                    out_ref[x, at, pl.ds((4 * h + q) * LANES, LANES)] = taken

    @pl.loop(0, CHUNKS // 4)
    def _(i):
        @pl.when(i < CHUNKS // 4 - 2)
        def _():
            for k in range(4):
                fetch(4 * i + 8 + k).start()

        for k in range(4):
            fetch(4 * i + k).wait()
        for k in range(5):
            if k < 4:
                permute(4 * i + k, k)
            if k > 0:
                gather(4 * i + k - 1, k - 1)


def relayout(line, core):
    return line.call(
        relayout_kernel,
        (struct((SLAB, NCORE, PLANE), BF16),),
        (core.reshape(NCORE * SLAB, PLANE),),
        specs=[pl.BlockSpec(memory_space=pltpu.HBM)],
        scratch=[
            pltpu.VMEM((CHUNKS, 256, PLANE), BF16),
            pltpu.VMEM((4, 4, 2, 256, LANES), F32),
            pltpu.VMEM((4, 256, 256), BF16),
            pltpu.SemaphoreType.DMA((CHUNKS,)),
        ],
        limit=42,
        micros=8,
    )[0]


def sums(field_of, core_ref, full_ref, half_ref):
    for x in range(SLAB):
        part = dot_nt(field_of(x), core_ref[x])
        if x == 0:
            full_ref[...] = part
        else:
            full_ref[...] += part
    half_ref[...] = full_ref[...].astype(BF16)


def map_kernel(counts, pick_ref, core_ref, *refs):
    sources, (out_ref, full_ref, half_ref) = refs[:-3], refs[-3:]
    perm = row_permutation(BATCH * SLAB, SLAB)
    for b, count in enumerate(counts):
        value = sources[0][...]
        if count == 2:
            odd = lax.axis_index("group") % 2 == 1
            value = jnp.where(odd, value, sources[1][...])
        sources = sources[count:]
        got = dot(dot(perm, value).astype(BF16), pick_ref[...]).astype(BF16)
        out_ref[:, b * BATCH : (b + 1) * BATCH, :] = got.reshape(SLAB, BATCH, PLANE)
    sums(lambda x: out_ref[x], core_ref, full_ref, half_ref)


def map_batches(line, pick, core_x, batches):
    rows = BATCH * len(batches)
    counts = tuple(len(b) for b in batches)
    flat = [a.reshape(BATCH * SLAB, PLANE) for b in batches for a in b]
    return line.call(
        lambda *refs: map_kernel(counts, *refs),
        (struct((SLAB, rows, PLANE), BF16), struct((rows, NCORE), F32), struct((rows, NCORE), BF16)),
        (pick, core_x, *flat),
        micros=2 + len(batches) // 2,
    )


def exchange(half):
    return [
        lax.ppermute(half, "grid", [(i, i ^ k) for i in range(GRID)]) for k in range(1, GRID)
    ]


def total_of(full_ref, a_ref, b_ref, c_ref):
    rest = a_ref[...].astype(F32) + b_ref[...].astype(F32) + c_ref[...].astype(F32)
    return (full_ref[...] + rest).astype(BF16)


def project_kernel(full_ref, a_ref, b_ref, c_ref, field_ref, core_ref, *refs):
    split_up = len(refs) == 6
    local_ref = refs[0] if split_up else None
    out_ref, halos = (refs[1], refs[2:]) if split_up else (refs[0], refs[1:])
    coef = total_of(full_ref, a_ref, b_ref, c_ref)
    for x in range(SLAB):
        value = field_ref[x].astype(F32) - dot(coef, core_ref[x])
        out_ref[x] = value
        sent = [value.astype(BF16)]
        if split_up:
            parts = [p.astype(F32) for p in split(local_ref[x : x + 1], 3)]
            rest = jnp.zeros((EXTRA - 4, PLANE), F32)
            extra = jnp.concatenate(parts + [jnp.ones((1, PLANE), F32), rest], axis=0)
            head = jnp.concatenate([sent[0][:BATCH], extra.astype(BF16)], axis=0)
            sent = [head, sent[0][BATCH:]]
        for k, short in enumerate(sent):
            if x < HALO:
                halos[2 * k][x] = short
            if x >= SLAB - HALO:
                halos[2 * k + 1][x - (SLAB - HALO)] = short


def project(line, full, others, field, core_x, local):
    rows = field.shape[1]
    sizes = [rows] if local is None else [BATCH + EXTRA, rows - BATCH]
    return line.call(
        project_kernel,
        (struct((SLAB, rows, PLANE), F32),)
        + tuple(struct((HALO, n, PLANE), BF16) for n in sizes for _ in range(2)),
        (full, *others, field, core_x) + ((local,) if local is not None else ()),
        micros=2,
    )


UP = [(i, i + 1) for i in range(GRID - 1)]
DOWN = [(j, i) for i, j in UP]


def filter_kernel(mode, offset, *refs):
    field_ref, below_ref, above_ref = refs[:3]
    others = ()
    if mode == "first":
        local_ref, weight_ref, first_ref, flag_ref, out_ref = refs[3:8]
    elif mode == "more":
        weight_ref, first_ref, flag_ref, out_ref = refs[3:7]
    else:
        weight_ref, first_ref, flag_ref, core_ref = refs[3:7]
        others, (out_ref, full_ref, half_ref) = refs[7:-7], refs[-7:-4]
    below, above, even, odd = refs[-4:]
    rows = BATCH
    if mode == "first":
        weight_ref[HALO : HALO + SLAB] = 8.0 * local_ref[...] - 2.0
        for k, ref in enumerate((below_ref, above_ref)):
            for x in range(HALO):
                extra = ref[x, rows : rows + EXTRA, :].astype(F32)
                near = (extra[0:1] + extra[1:2]) + extra[2:3]
                place = x if k == 0 else HALO + SLAB + x
                weight_ref[place : place + 1] = 8.0 * near - 2.0
                if x == 0:
                    flag_ref[k] = jnp.broadcast_to(extra[3:4, :LANES], (8, LANES))
        first_ref[...] = weight_ref[...] - EK[KDEG - 1]
    lane = iota((8, LANES), 1)
    head, tail = lane < 16, lane >= LANES - 16
    first_z, last_z = lane % 16 == 0, lane % 16 == 15
    low_flag, high_flag = flag_ref[0], flag_ref[1]

    def rolled(mask, value, by):
        return pltpu.roll(jnp.where(mask, 0.0, value), by % LANES, 1)

    def sweep(local, at, put):
        def begin(x, lanes):
            if x < HALO:
                return below[x, local, lanes]
            if x >= HALO + SLAB:
                return above[x - HALO - SLAB, local, lanes]
            return field_ref[x - HALO, at, lanes]

        def tiles(source, x):
            every = [pl.ds(j * LANES, LANES) for j in range(TILES)]
            if source is None:
                return [begin(x, lanes) for lanes in every]
            return [source[x, :, lanes] for lanes in every]

        source = None
        for k in range(1, KDEG + 1):
            target = even if k % 2 == 0 else odd
            first, last = k, WIDE - k
            here, after = tiles(source, first - 1), tiles(source, first)
            for x in range(first, last):
                before, here = here, after
                after = tiles(source, x + 1)
                up = [rolled(head, here[j], -16) for j in range(2)]
                down = [rolled(tail, here[j], 16) for j in range(6, 8)]
                for j in range(TILES):
                    lanes = pl.ds(j * LANES, LANES)
                    c = here[j]
                    above_y = here[j + 2] if j < 6 else up[j - 6]
                    below_y = here[j - 2] if j > 1 else down[j]
                    mate = here[j ^ 1]
                    z = mate + (rolled(first_z, mate, -1) if j % 2 else rolled(last_z, mate, 1))
                    around = (before[j] + after[j]) + (above_y + below_y) + z
                    w_ref = first_ref if k == 1 else weight_ref
                    w = jnp.broadcast_to(w_ref[pl.ds(x, 1), lanes], (8, LANES))
                    value = around - w * c
                    if k > 1:
                        value = value + EK[KDEG - k] * begin(x, lanes)
                    if x == HALO - 1:
                        value = value * low_flag
                    elif x == HALO + SLAB:
                        value = value * high_flag
                    if k == KDEG:
                        out_ref[x - HALO, put, lanes] = value * TOP
                    else:
                        target[x, :, lanes] = value
            source = target

    @pl.loop(0, out_ref.shape[1] // 16)
    def _(i):
        both = pl.ds(pl.multiple_of(i * 16, 16), 16)
        below[...] = below_ref[:, both, :].astype(F32)
        above[...] = above_ref[:, both, :].astype(F32)

        @pl.loop(0, 2)
        def _(k):
            sweep(
                pl.ds(pl.multiple_of(k * 8, 8), 8),
                pl.ds(pl.multiple_of(offset + i * 16 + k * 8, 8), 8),
                pl.ds(pl.multiple_of(i * 16 + k * 8, 8), 8),
            )

    if mode == "last":

        def all_of(x):
            return jnp.concatenate([r[x].astype(BF16) for r in (*others, out_ref)], axis=0)

        sums(all_of, core_ref, full_ref, half_ref)


def filter_scratch():
    halo, whole = pltpu.VMEM((HALO, 16, PLANE), F32), pltpu.VMEM((WIDE, 8, PLANE), F32)
    return [halo, halo, whole, whole]


def filter_first(line, field, below, above, local):
    wide = struct((WIDE, PLANE), F32)
    got = line.call(
        lambda *refs: filter_kernel("first", 0, *refs),
        (wide, wide, struct((2, 8, LANES), F32), struct((SLAB, BATCH, PLANE), F32)),
        (field, below, above, local),
        scratch=filter_scratch(),
        micros=6,
    )
    return got[:3], got[3]


def filter_more(line, field, below, above, weight):
    return line.call(
        lambda *refs: filter_kernel("more", BATCH, *refs),
        (struct((SLAB, BATCH, PLANE), F32),),
        (field, below, above, *weight),
        scratch=filter_scratch(),
        micros=6,
    )[0]


def filter_last(line, field, below, above, weight, core_x, others):
    total = BATCH * (1 + len(others))
    return line.call(
        lambda *refs: filter_kernel("last", 0, *refs),
        (struct((SLAB, BATCH, PLANE), F32), struct((total, NCORE), F32), struct((total, NCORE), BF16)),
        (field, below, above, *weight, core_x, *others),
        scratch=filter_scratch(),
        micros=8,
    )


def reorder(value, order_ref):
    parts = split(value, 2)
    return dot(parts[0], order_ref[...]) + dot(parts[1], order_ref[...])


def clean_kernel(full_ref, a_ref, b_ref, c_ref, first_ref, more_ref, last_ref, mapped_ref, mapped_rest_ref, core_ref, order_ref, own_ref, density_ref, own, rows):
    coef = total_of(full_ref, a_ref, b_ref, c_ref)
    for x in range(SLAB):
        taken = dot(coef, core_ref[x])
        mapped = (mapped_ref[x, :BATCH], mapped_ref[x, BATCH:], mapped_rest_ref[x])
        total = None
        for t, ref in enumerate((first_ref, more_ref, last_ref)):
            value = ref[x] - taken[t * BATCH : (t + 1) * BATCH]
            if t == 0:
                own[x * BATCH : (x + 1) * BATCH] = value
            term = mapped[t].astype(F32) * value
            total = term if total is None else total + term
        rows[x : x + 1] = jnp.sum(total, axis=0, keepdims=True) / (3.0 * BATCH)
    back = row_permutation(BATCH * SLAB, BATCH)
    total = None
    for part in split(own[...], 2):
        moved = dot(dot(back, part).astype(BF16), order_ref[...])
        total = moved if total is None else total + moved
    own_ref[...] = total
    density_ref[...] = reorder(rows[...], order_ref)


def clean(line, full, others, fields, mapped, mapped_rest, core_x, order):
    small, own = struct((SLAB, PLANE), F32), struct((SLAB * BATCH, PLANE), F32)
    return line.call(
        clean_kernel,
        (own, small),
        (full, *others, *fields, mapped, mapped_rest, core_x, order),
        scratch=[pltpu.VMEM(own.shape, F32), pltpu.VMEM(small.shape, F32)],
        limit=12,
        micros=4,
    )


def permute_groups(array, pairs):
    return lax.ppermute(array, "group", pairs)


def body(stochastic, plane_map, core_orbitals, potential):
    groups = lax.axis_size("group")
    mate = permute_groups(stochastic, [(i, i ^ 1) for i in range(groups)])
    third = permute_groups(stochastic, [(i, (i + 2) % groups) for i in range(groups)])

    line = Line()
    core_x = relayout(line, core_orbitals[0])
    order, pick, local = prepare(line, plane_map, potential[0])

    mate, line.token = lax.optimization_barrier((mate, line.token))
    second = permute_groups(mate, [(i, (i + 2) % groups) for i in range(0, groups, 2)])
    mapped, full, half = map_batches(line, pick, core_x, [(stochastic,), (third,)])
    others = exchange(half)
    field, low, high, low_more, high_more = project(line, full, others, mapped, core_x, local)
    below = lax.ppermute(high, "grid", UP)
    above = lax.ppermute(low, "grid", DOWN)

    mapped_rest, full, half = map_batches(line, pick, core_x, [(mate, second)])
    others = exchange(half)
    below_more = lax.ppermute(high_more, "grid", UP)
    above_more = lax.ppermute(low_more, "grid", DOWN)
    weight, first = filter_first(line, field, below, above, local)
    rest, low, high = project(line, full, others, mapped_rest, core_x, None)
    below_rest = lax.ppermute(high, "grid", UP)
    above_rest = lax.ppermute(low, "grid", DOWN)
    more = filter_more(line, field, below_more, above_more, weight)
    last, full, half = filter_last(
        line, rest, below_rest, above_rest, weight, core_x, (first, more)
    )
    fields = (first, more, last)
    own, density = clean(line, full, exchange(half), fields, mapped, mapped_rest, core_x, order)
    return density[None], own.reshape(BATCH, SLAB, PLANE)


def solution(mesh):
    return jax.shard_map(
        body,
        mesh=mesh,
        in_specs=(
            P("group", "grid", None),
            P("group", None),
            P("group", None, "grid", None),
            P("group", "grid", None),
        ),
        out_specs=(P("group", "grid", None), P("group", "grid", None)),
        check_vma=False,
    )
```

```python
from fractions import Fraction

import jax
import jax.numpy as jnp
from jax import lax
from jax.experimental import pallas as pl
from jax.experimental.pallas import tpu as pltpu
from jax.sharding import PartitionSpec as P


BZ = 32
KDEG = 6
BATCH = 32
NCORE = 512
SLAB = 8
PLANE = 1024
GRID = 4
HALO = KDEG
WIDE = SLAB + 2 * HALO
LANES = 128
TILES = PLANE // LANES
F32 = jnp.float32
BF16 = jnp.bfloat16


def horner_coefficients():
    cheb = [[Fraction(1)], [Fraction(0), Fraction(1)]]
    for _ in range(2, KDEG + 1):
        last, before = cheb[-1], cheb[-2]
        nxt = [Fraction(0)] + [2 * v for v in last]
        for i, v in enumerate(before):
            nxt[i] -= v
        cheb.append(nxt)
    mono = [Fraction(0)] * (KDEG + 1)
    for k, poly in enumerate(cheb):
        for i, v in enumerate(poly):
            mono[i] += v / (k + 1)
    scaled = [v / Fraction(-8) ** i for i, v in enumerate(mono)]
    top = scaled[KDEG]
    return [float(v / top) for v in scaled], float(top)


EK, TOP = horner_coefficients()

VMEM = pl.BlockSpec(memory_space=pltpu.VMEM)
ANY = pl.BlockSpec(memory_space=pl.ANY)
MIB = 1 << 20
PIECE = 32
SCALE = 500e6
EXTRA = 8
CHUNKS = NCORE // PIECE
NT = (((1,), (1,)), ((), ()))


class Line:
    def __init__(self):
        self.token = None

    def call(self, kernel, out_shape, args, specs=None, scratch=(), limit=8, micros=2):
        specs = list(specs or [VMEM] * len(args))
        args = list(args)
        waits = self.token is not None
        if waits:
            args.append(self.token)
            specs.append(ANY)
        outs = tuple(out_shape) + (struct((8, LANES), F32),)

        def with_token(*refs):
            ins, rest = refs[: len(args)], refs[len(args) :]
            mine, token, extra = rest[: len(outs) - 1], rest[len(outs) - 1], rest[len(outs) :]
            kernel(*ins[: len(args) - waits], *mine, *extra)
            token[...] = jnp.zeros((8, LANES), F32)

        got = pl.pallas_call(
            with_token,
            in_specs=specs,
            out_specs=tuple(VMEM for _ in outs),
            out_shape=outs,
            scratch_shapes=list(scratch),
            compiler_params=pltpu.CompilerParams(vmem_limit_bytes=limit * MIB),
            cost_estimate=pl.CostEstimate(
                flops=int(micros * SCALE), bytes_accessed=1024, transcendentals=0
            ),
        )(*args)
        self.token = got[-1]
        return got[:-1]


def struct(shape, dtype):
    return jax.ShapeDtypeStruct(shape, dtype)


def one_hot(condition):
    return jnp.where(condition, 1.0, 0.0).astype(BF16)


def iota(shape, axis):
    return lax.broadcasted_iota(jnp.int32, shape, axis)


def dot(a, b):
    return jnp.dot(a, b, preferred_element_type=F32)


def dot_nt(a, b):
    return lax.dot_general(a, b, NT, preferred_element_type=F32)


def split(value, parts):
    out = []
    for _ in range(parts):
        out.append(value.astype(BF16))
        value = value - out[-1].astype(F32)
    return out


def row_permutation(rows, inner):
    outer = rows // inner
    out, src = iota((rows, rows), 0), iota((rows, rows), 1)
    return one_hot(src == (out % outer) * inner + out // outer)


def natural_point(q):
    tile, lane = q // LANES, q % LANES
    return (4 * (lane // 16) + tile // 2) * BZ + 2 * (lane % 16) + tile % 2


def prepare_kernel(index_ref, local_ref, order_ref, pick_ref, local_out):
    order_ref[...] = one_hot(iota((PLANE, PLANE), 1) == natural_point(iota((PLANE, PLANE), 0)))
    index = index_ref[...]
    digits = jnp.concatenate([index // 32, index % 32] + [jnp.zeros((6, PLANE), jnp.int32)], axis=0)
    rows = jnp.concatenate([digits.astype(F32)] + [p.astype(F32) for p in split(local_ref[...], 3)], axis=0)
    moved = dot_nt(rows.astype(BF16), order_ref[...])
    local_out[...] = (moved[8:16] + moved[16:24]) + moved[24:32]
    index = (moved[0:1] * 32.0 + moved[1:2]).astype(jnp.int32)
    pick_ref[...] = one_hot(iota((PLANE, PLANE), 0) == index)


def prepare(line, plane_map, local):
    square = struct((PLANE, PLANE), BF16)
    return line.call(
        prepare_kernel, (square, square, struct((SLAB, PLANE), F32)), (plane_map, local), micros=2
    )


def relayout_kernel(core_hbm, out_ref, raw, wide, columns_ref, sems):
    def fetch(i):
        return pltpu.make_async_copy(core_hbm.at[pl.ds(i * 256, 256), :], raw.at[i], sems.at[i])

    for i in range(8):
        fetch(i).start()
    src, out = iota((256, 256), 0), iota((256, 256), 1)
    for b in range(4):
        piece, low = 4 * (out // LANES) + (out // PIECE - b) % 4, out % PIECE
        columns_ref[b] = one_hot(
            src == (4 * (low // 16) + piece // 2) * BZ + 2 * (low % 16) + piece % 2
        )
    quarter = iota((PIECE, LANES), 1) // PIECE

    def permute(i, k):
        for b in range(4):
            moved = dot(raw[i, :, pl.ds(b * 256, 256)], columns_ref[b])
            wide[k, b, 0] = moved[:, :LANES]
            wide[k, b, 1] = moved[:, LANES:]

    def gather(i, k):
        at = pl.ds(pl.multiple_of(i * PIECE, PIECE), PIECE)
        for x in range(SLAB):
            rows = pl.ds(x, PIECE, stride=SLAB)
            for h in range(2):
                p = [wide[k, b, h, rows, :].astype(BF16) for b in range(4)]
                for q in range(4):
                    taken = p[3]
                    for b in range(3):
                        taken = jnp.where(quarter == (q + b) % 4, p[b], taken)
                    if q:
                        taken = pltpu.roll(taken, LANES - q * PIECE, 1)
                    out_ref[x, at, pl.ds((4 * h + q) * LANES, LANES)] = taken

    @pl.loop(0, CHUNKS // 4)
    def _(i):
        @pl.when(i < CHUNKS // 4 - 2)
        def _():
            for k in range(4):
                fetch(4 * i + 8 + k).start()

        for k in range(4):
            fetch(4 * i + k).wait()
        for k in range(5):
            if k < 4:
                permute(4 * i + k, k)
            if k > 0:
                gather(4 * i + k - 1, k - 1)


def relayout(line, core):
    return line.call(
        relayout_kernel,
        (struct((SLAB, NCORE, PLANE), BF16),),
        (core.reshape(NCORE * SLAB, PLANE),),
        specs=[pl.BlockSpec(memory_space=pltpu.HBM)],
        scratch=[
            pltpu.VMEM((CHUNKS, 256, PLANE), BF16),
            pltpu.VMEM((4, 4, 2, 256, LANES), F32),
            pltpu.VMEM((4, 256, 256), BF16),
            pltpu.SemaphoreType.DMA((CHUNKS,)),
        ],
        limit=42,
        micros=8,
    )[0]


def sums(field_of, core_ref, full_ref, half_ref):
    for x in range(SLAB):
        part = dot_nt(field_of(x), core_ref[x])
        if x == 0:
            full_ref[...] = part
        else:
            full_ref[...] += part
    half_ref[...] = full_ref[...].astype(BF16)


def map_kernel(counts, pick_ref, core_ref, *refs):
    sources, (out_ref, full_ref, half_ref) = refs[:-3], refs[-3:]
    perm = row_permutation(BATCH * SLAB, SLAB)
    for b, count in enumerate(counts):
        value = sources[0][...]
        if count == 2:
            odd = lax.axis_index("group") % 2 == 1
            value = jnp.where(odd, value, sources[1][...])
        sources = sources[count:]
        got = dot(dot(perm, value).astype(BF16), pick_ref[...]).astype(BF16)
        out_ref[:, b * BATCH : (b + 1) * BATCH, :] = got.reshape(SLAB, BATCH, PLANE)
    sums(lambda x: out_ref[x], core_ref, full_ref, half_ref)


def map_batches(line, pick, core_x, batches):
    rows = BATCH * len(batches)
    counts = tuple(len(b) for b in batches)
    flat = [a.reshape(BATCH * SLAB, PLANE) for b in batches for a in b]
    return line.call(
        lambda *refs: map_kernel(counts, *refs),
        (struct((SLAB, rows, PLANE), BF16), struct((rows, NCORE), F32), struct((rows, NCORE), BF16)),
        (pick, core_x, *flat),
        micros=2 + len(batches) // 2,
    )


def exchange(half):
    return [
        lax.ppermute(half, "grid", [(i, i ^ k) for i in range(GRID)]) for k in range(1, GRID)
    ]


def total_of(full_ref, a_ref, b_ref, c_ref):
    rest = a_ref[...].astype(F32) + b_ref[...].astype(F32) + c_ref[...].astype(F32)
    return (full_ref[...] + rest).astype(BF16)


def project_kernel(full_ref, a_ref, b_ref, c_ref, field_ref, core_ref, *refs):
    local_ref = refs[0] if len(refs) == 4 else None
    out_ref, low_ref, high_ref = refs[-3:]
    coef = total_of(full_ref, a_ref, b_ref, c_ref)
    for x in range(SLAB):
        value = field_ref[x].astype(F32) - dot(coef, core_ref[x])
        out_ref[x] = value
        short = value.astype(BF16)
        if local_ref is not None:
            parts = [p.astype(F32) for p in split(local_ref[x : x + 1], 3)]
            rest = jnp.zeros((EXTRA - 4, PLANE), F32)
            extra = jnp.concatenate(parts + [jnp.ones((1, PLANE), F32), rest], axis=0)
            short = jnp.concatenate([short, extra.astype(BF16)], axis=0)
        if x < HALO:
            low_ref[x] = short
        if x >= SLAB - HALO:
            high_ref[x - (SLAB - HALO)] = short


def project(line, full, others, field, core_x, local):
    rows = field.shape[1]
    sent = rows + (EXTRA if local is not None else 0)
    return line.call(
        project_kernel,
        (
            struct((SLAB, rows, PLANE), F32),
            struct((HALO, sent, PLANE), BF16),
            struct((HALO, sent, PLANE), BF16),
        ),
        (full, *others, field, core_x) + ((local,) if local is not None else ()),
        micros=2,
    )


UP = [(i, i + 1) for i in range(GRID - 1)]
DOWN = [(j, i) for i, j in UP]


def filter_kernel(ahead, *refs):
    field_ref, below_ref, above_ref = refs[:3]
    if ahead:
        local_ref, weight_ref, first_ref, flag_ref, out_ref = refs[3:8]
    else:
        weight_ref, first_ref, flag_ref, core_ref, other_ref, out_ref, full_ref, half_ref = refs[3:11]
    below, above, even, odd = refs[-4:]
    rows = field_ref.shape[1]
    if ahead:
        weight_ref[HALO : HALO + SLAB] = 8.0 * local_ref[...] - 2.0
        for k, ref in enumerate((below_ref, above_ref)):
            for x in range(HALO):
                extra = ref[x, rows : rows + EXTRA, :].astype(F32)
                near = (extra[0:1] + extra[1:2]) + extra[2:3]
                place = x if k == 0 else HALO + SLAB + x
                weight_ref[place : place + 1] = 8.0 * near - 2.0
                if x == 0:
                    flag_ref[k] = jnp.broadcast_to(extra[3:4, :LANES], (8, LANES))
        first_ref[...] = weight_ref[...] - EK[KDEG - 1]
    lane = iota((8, LANES), 1)
    head, tail = lane < 16, lane >= LANES - 16
    first_z, last_z = lane % 16 == 0, lane % 16 == 15
    low_flag, high_flag = flag_ref[0], flag_ref[1]

    def rolled(mask, value, by):
        return pltpu.roll(jnp.where(mask, 0.0, value), by % LANES, 1)

    def sweep(local, at):
        def begin(x, lanes):
            if x < HALO:
                return below[x, local, lanes]
            if x >= HALO + SLAB:
                return above[x - HALO - SLAB, local, lanes]
            return field_ref[x - HALO, at, lanes]

        def tiles(source, x):
            every = [pl.ds(j * LANES, LANES) for j in range(TILES)]
            if source is None:
                return [begin(x, lanes) for lanes in every]
            return [source[x, :, lanes] for lanes in every]

        source = None
        for k in range(1, KDEG + 1):
            target = even if k % 2 == 0 else odd
            first, last = k, WIDE - k
            here, after = tiles(source, first - 1), tiles(source, first)
            for x in range(first, last):
                before, here = here, after
                after = tiles(source, x + 1)
                up = [rolled(head, here[j], -16) for j in range(2)]
                down = [rolled(tail, here[j], 16) for j in range(6, 8)]
                for j in range(TILES):
                    lanes = pl.ds(j * LANES, LANES)
                    c = here[j]
                    above_y = here[j + 2] if j < 6 else up[j - 6]
                    below_y = here[j - 2] if j > 1 else down[j]
                    mate = here[j ^ 1]
                    z = mate + (rolled(first_z, mate, -1) if j % 2 else rolled(last_z, mate, 1))
                    around = (before[j] + after[j]) + (above_y + below_y) + z
                    w_ref = first_ref if k == 1 else weight_ref
                    w = jnp.broadcast_to(w_ref[pl.ds(x, 1), lanes], (8, LANES))
                    value = around - w * c
                    if k > 1:
                        value = value + EK[KDEG - k] * begin(x, lanes)
                    if x == HALO - 1:
                        value = value * low_flag
                    elif x == HALO + SLAB:
                        value = value * high_flag
                    if k == KDEG:
                        out_ref[x - HALO, at, lanes] = value * TOP
                    else:
                        target[x, :, lanes] = value
            source = target

    @pl.loop(0, rows // 16)
    def _(i):
        both = pl.ds(pl.multiple_of(i * 16, 16), 16)
        below[...] = below_ref[:, both, :].astype(F32)
        above[...] = above_ref[:, both, :].astype(F32)

        @pl.loop(0, 2)
        def _(k):
            sweep(
                pl.ds(pl.multiple_of(k * 8, 8), 8),
                pl.ds(pl.multiple_of(i * 16 + k * 8, 8), 8),
            )

    if not ahead:

        def both_of(x):
            return jnp.concatenate([other_ref[x].astype(BF16), out_ref[x].astype(BF16)], axis=0)

        sums(both_of, core_ref, full_ref, half_ref)


def filter_scratch():
    halo, whole = pltpu.VMEM((HALO, 16, PLANE), F32), pltpu.VMEM((WIDE, 8, PLANE), F32)
    return [halo, halo, whole, whole]


def filter_ahead(line, field, below, above, local):
    rows = field.shape[1]
    wide = struct((WIDE, PLANE), F32)
    got = line.call(
        lambda *refs: filter_kernel(True, *refs),
        (wide, wide, struct((2, 8, LANES), F32), struct((SLAB, rows, PLANE), F32)),
        (field, below, above, local),
        scratch=filter_scratch(),
        micros=7,
    )
    return got[:3], got[3]


def filter_rest(line, field, below, above, weight, core_x, ahead):
    rows = field.shape[1]
    total = rows + ahead.shape[1]
    return line.call(
        lambda *refs: filter_kernel(False, *refs),
        (struct((SLAB, rows, PLANE), F32), struct((total, NCORE), F32), struct((total, NCORE), BF16)),
        (field, below, above, *weight, core_x, ahead),
        scratch=filter_scratch(),
        micros=14,
    )


def reorder(value, order_ref):
    parts = split(value, 2)
    return dot(parts[0], order_ref[...]) + dot(parts[1], order_ref[...])


def clean_kernel(full_ref, a_ref, b_ref, c_ref, ahead_ref, rest_ref, mapped_ref, mapped_rest_ref, core_ref, order_ref, own_ref, density_ref, own, rows):
    coef = total_of(full_ref, a_ref, b_ref, c_ref)
    for x in range(SLAB):
        taken = dot(coef, core_ref[x])
        ahead = ahead_ref[x] - taken[:BATCH]
        rest = rest_ref[x] - taken[BATCH:]
        own[x * BATCH : (x + 1) * BATCH] = ahead
        weighted = jnp.sum(mapped_ref[x].astype(F32) * ahead, axis=0, keepdims=True)
        weighted += jnp.sum(mapped_rest_ref[x].astype(F32) * rest, axis=0, keepdims=True)
        rows[x : x + 1] = weighted / (3.0 * BATCH)
    back = row_permutation(BATCH * SLAB, BATCH)
    total = None
    for part in split(own[...], 2):
        moved = dot(dot(back, part).astype(BF16), order_ref[...])
        total = moved if total is None else total + moved
    own_ref[...] = total
    density_ref[...] = reorder(rows[...], order_ref)


def clean(line, full, others, ahead, rest, mapped, mapped_rest, core_x, order):
    small, own = struct((SLAB, PLANE), F32), struct((SLAB * BATCH, PLANE), F32)
    return line.call(
        clean_kernel,
        (own, small),
        (full, *others, ahead, rest, mapped, mapped_rest, core_x, order),
        scratch=[pltpu.VMEM(own.shape, F32), pltpu.VMEM(small.shape, F32)],
        limit=12,
        micros=4,
    )


def permute_groups(array, pairs):
    return lax.ppermute(array, "group", pairs)


def body(stochastic, plane_map, core_orbitals, potential):
    groups = lax.axis_size("group")
    mate = permute_groups(stochastic, [(i, i ^ 1) for i in range(groups)])
    third = permute_groups(stochastic, [(i, (i + 2) % groups) for i in range(groups)])

    line = Line()
    core_x = relayout(line, core_orbitals[0])
    order, pick, local = prepare(line, plane_map, potential[0])

    mate, line.token = lax.optimization_barrier((mate, line.token))
    second = permute_groups(mate, [(i, (i + 2) % groups) for i in range(0, groups, 2)])
    mapped, full, half = map_batches(line, pick, core_x, [(stochastic,)])
    others = exchange(half)
    field, low, high = project(line, full, others, mapped, core_x, local)
    below = lax.ppermute(high, "grid", UP)
    above = lax.ppermute(low, "grid", DOWN)

    batches = [(third,), (mate, second)]
    mapped_rest, full, half = map_batches(line, pick, core_x, batches)
    rest, low, high = project(line, full, exchange(half), mapped_rest, core_x, None)
    below_rest, above_rest = lax.ppermute(high, "grid", UP), lax.ppermute(low, "grid", DOWN)

    weight, ahead = filter_ahead(line, field, below, above, local)
    rest, full, half = filter_rest(line, rest, below_rest, above_rest, weight, core_x, ahead)
    own, density = clean(
        line, full, exchange(half), ahead, rest, mapped, mapped_rest, core_x, order
    )
    return density[None], own.reshape(BATCH, SLAB, PLANE)


def solution(mesh):
    return jax.shard_map(
        body,
        mesh=mesh,
        in_specs=(
            P("group", "grid", None),
            P("group", None),
            P("group", None, "grid", None),
            P("group", "grid", None),
        ),
        out_specs=(P("group", "grid", None), P("group", "grid", None)),
        check_vma=False,
    )
```
